256 devices in a mesh: seq: 4 (over x), row: 2 (over core), col: 32 (over z, y).
Axes of the slice: x: 4, y: 4, z: 8, core: 2. Of those that a mesh axis runs over, the one named last changes fastest.
Arguments:
- activations: bfloat16 [2048, 16384], P('seq', ('row', 'col')), may hold values from -1500 to 1500
- norm_gain: float32 [16384], P(('row', 'col')), may hold values from 0.1 to 1.9
- query_weight: bfloat16 [16384, 8192], P('row', 'col'), may hold values from -0.046875 to 0.046875
- kv_weight: bfloat16 [16384, 2, 512], P('row'), may hold values from -0.046875 to 0.046875
- out_weight: bfloat16 [8192, 16384], P('col', 'row'), may hold values from -0.5 to 0.5
- block_ids: int32 [2048], replicated, may hold values from 0 to 255, never falling along the last dimension, each value on 1 to 16 neighbouring positions
- clean_mask: int32 [2048], replicated, may hold values 0 or 1
Outputs:
- layer_out: bfloat16 [2048, 16384], P('seq', ('row', 'col'))
The draws below stay inside these ranges and needn't reach their ends.
Inputs may be any that keep to these rules, and one draw needn't show every extreme that they name: `block_ids`: block numbers never fall along the sequence; every block holds 1 to 16 tokens and one holds exactly 16.
All inputs are finite; a program needn't handle non-finite values.
Results may differ from the reference program's by a relative error of at most 0.009.
Values may be sent and summed in bfloat16 or wider, within the bound.
A program may use at most 128 MiB of HBM per device.

```python
import math
import jax
import jax.numpy as jnp
import numpy as np
from jax import lax

D = 16384
HD = 128
QH = 64
KVH = 4
BMAX = 16
LEN = 2048
NBLK = 256


def draw_activations(key, part):
    row_key, col_key, base_key = jax.random.split(key, 3)
    column_ramp = jnp.arange(D, dtype=jnp.float32) / max(D - 1, 1)
    col_scale = jnp.exp(jax.random.uniform(col_key, (1, D), dtype=jnp.float32) * math.log(10.0) + math.log(3.0) * column_ramp[None, :])
    row_scale = jnp.exp(jax.random.uniform(row_key, (LEN, 1), dtype=jnp.float32) * math.log(10.0))
    base_draw = jax.random.truncated_normal(base_key, -4.0, 4.0, (LEN, D), dtype=jnp.float32)
    return (base_draw * row_scale * col_scale).astype(jnp.bfloat16)


def touch_ends(entries, rng, low, high):
    shape = entries.shape
    place = [jax.random.randint(jax.random.fold_in(rng, axis), (), 0, shape[axis]) for axis in range(len(shape))]
    entries = entries.at[tuple(place)].set(low)
    longest = shape.index(max(shape))
    place[longest] = (place[longest] + 1) % shape[longest]
    return entries.at[tuple(place)].set(high)


def levels(rng, dims, cuts, low, top_value):
    loudness, own = 1.0, jax.random.fold_in(rng, 6)
    for dim, shards_of in cuts:
        draws = jnp.exp(jax.random.uniform(jax.random.fold_in(own, dim), (shards_of,), jnp.float32, low / len(cuts), top_value / len(cuts)))
        loudness = loudness * jnp.repeat(draws, dims[dim] // shards_of).reshape([-1 if axis == dim else 1 for axis in range(len(dims))])
    return loudness


def length_profile(amount, total, most, lean):
    portions = [(1 << 20) // math.isqrt(rank ** lean) + 1 for rank in range(2, amount + 1)]
    surplus, counts = total - most - (amount - 1), [1] * (amount - 1)
    while surplus > 0:
        free = [i for i in range(amount - 1) if counts[i] < most]
        whole, remaining = sum([portions[i] for i in free]), surplus
        for i in free:
            addition = min(most - counts[i], max(1, remaining * portions[i] // whole), surplus)
            counts[i] = counts[i] + addition
            surplus = surplus - addition
    return np.array([most] + counts)


def ragged(own_key, number_of, total, bound, skew):
    if number_of == 2:
        one = jax.random.randint(own_key, (), max(1, total - bound), min(bound, total - 1) + 1)
        return jnp.stack([one, total - one])
    sizes = jnp.asarray(length_profile(number_of, total, bound, skew), jnp.int32)
    pairs = (number_of - 1) // 2
    source_of, receiver = sizes[1:1 + 2 * pairs:2], sizes[2:2 + 2 * pairs:2]
    margin = jnp.minimum(source_of - 1, bound - receiver)
    passed = jax.random.randint(jax.random.fold_in(own_key, 1), (pairs,), 0, 1 << 20) % (margin + 1)
    sizes = sizes.at[1:1 + 2 * pairs:2].set(source_of - passed).at[2:2 + 2 * pairs:2].set(receiver + passed)
    return sizes[jax.random.permutation(jax.random.fold_in(own_key, 2), number_of)]


def centred(rng, extent, scale, bound, cuts=(), kind=jnp.bfloat16):
    values = scale * jax.random.normal(rng, extent, jnp.float32)
    if cuts:
        values = values * levels(rng, extent, cuts, -0.22, 0.18)
    return jnp.clip(values, -bound, bound).astype(kind)


def setup_inputs(seed: int = 0) -> dict:
    keys = jax.random.split(jax.random.key(seed), 8)
    activations = draw_activations(jax.random.fold_in(keys[7], 71), 0)
    norm_gain = jnp.clip(1.0 + 0.18 * jax.random.normal(keys[1], (D,), jnp.float32), 0.1, 1.9)
    query_weight = centred(keys[2], (D, QH * HD), D ** -0.5, 0.046875, ((0, 2), (1, 32)))
    kv_weight = centred(keys[3], (D, 2, KVH * HD), D ** -0.5, 0.046875, ((0, 2),))
    out_weight = centred(keys[4], (QH * HD, D), HD ** -0.5, 0.5, ((0, 32), (1, 2)))
    block_ids = jnp.searchsorted(jnp.cumsum(ragged(keys[5], NBLK, LEN, BMAX, 1)), jnp.arange(LEN), side="right").astype(jnp.int32)
    clean_mask = touch_ends((jax.random.randint(keys[6], (LEN,), 0, 2) < 1).astype(jnp.int32), jax.random.fold_in(keys[6], 1), 0, 1)
    return {"activations": activations, "norm_gain": norm_gain, "query_weight": query_weight, "kv_weight": kv_weight, "out_weight": out_weight, "block_ids": block_ids, "clean_mask": clean_mask}


rope_base = 500000.0
norm_eps = 1e-05

def rotate(values, positions):
    half_dim = values.shape[-1] // 2
    inverse = jnp.exp(jnp.arange(half_dim, dtype=jnp.float32) * (-2.0 * math.log(rope_base) / values.shape[-1]))
    angles = positions.astype(jnp.float32)[:, None] * inverse[None, :]
    cosine = jnp.cos(angles)
    sine_part = jnp.sin(angles)
    first_half = values[..., :half_dim]
    second_half = values[..., half_dim:]
    return jnp.concatenate([first_half * cosine - second_half * sine_part, second_half * cosine + first_half * sine_part], axis=-1)

def reference(activations, norm_gain, query_weight, kv_weight, out_weight, block_ids, clean_mask):
    wide_input = activations.astype(jnp.float32)
    scaling = lax.rsqrt(lax.optimization_barrier(jnp.sum(wide_input * wide_input, axis=1)) / D + norm_eps)
    normed = (wide_input * scaling[:, None] * norm_gain[None, :]).astype(jnp.bfloat16)
    positions = jnp.arange(LEN, dtype=jnp.int32)
    query_raw = jnp.dot(normed, query_weight, preferred_element_type=jnp.float32).reshape(LEN, QH, HD).transpose(1, 0, 2)
    queries = rotate(query_raw, positions).astype(jnp.bfloat16)
    kv_raw = jnp.dot(normed, kv_weight.reshape(D, 2 * KVH * HD), preferred_element_type=jnp.float32).reshape(LEN, 2, KVH, HD)
    key_rows = rotate(kv_raw[:, 0].transpose(1, 0, 2), positions).astype(jnp.bfloat16)
    value_rows = kv_raw[:, 1].transpose(1, 0, 2).astype(jnp.bfloat16)
    own_block = block_ids[:, None]
    key_block = block_ids[None, :]
    visible = (key_block == own_block) | (key_block < own_block) & (clean_mask[None, :] == 1)
    group_size = QH // KVH
    score_scale = 1.0 / math.sqrt(HD)

    def one_head(head_index):
        query_head = lax.dynamic_index_in_dim(queries, head_index, 0, keepdims=False)
        kv_index = head_index // group_size
        key_head = lax.dynamic_index_in_dim(key_rows, kv_index, 0, keepdims=False)
        value_head = lax.dynamic_index_in_dim(value_rows, kv_index, 0, keepdims=False)
        scores = jnp.dot(query_head, key_head.T, preferred_element_type=jnp.float32) * score_scale
        weights = jnp.where(visible, jnp.exp(scores), jnp.zeros_like(scores))
        totals = lax.optimization_barrier(jnp.sum(weights, axis=1))
        summed = jnp.dot(weights.astype(jnp.bfloat16), value_head, preferred_element_type=jnp.float32)
        return (summed / totals[:, None]).astype(jnp.bfloat16)
    attended = lax.map(one_head, jnp.arange(QH, dtype=jnp.int32))
    merged = attended.transpose(1, 0, 2).reshape(LEN, QH * HD)
    return jnp.dot(merged, out_weight, preferred_element_type=jnp.float32).astype(jnp.bfloat16)
```

```python
import heapq
import math

import jax
import jax.numpy as jnp
import numpy as np
from jax import lax
from jax.experimental import pallas as pl
from jax.experimental.pallas import tpu as pltpu
from jax.sharding import PartitionSpec as P

D = 16384
HD = 128
QH = 64
KVH = 4
rope_base = 500000.0
norm_eps = 1e-05

MESH = pl.DeviceIdType.MESH
F32 = jnp.float32
BF16 = jnp.bfloat16

NZ, NY = 8, 4
SLAB = 512
SPLIT = 208
ROWS = ((0, SPLIT), (SPLIT, SLAB - SPLIT))
CH = 256


def norm(n):
    return (n[0] % NZ, n[1] % NY)


def slot(n):
    return (n[0] % NZ) * NY + n[1] % NY


def make_tree(part):
    parent = {}

    def ring(start, axis, size, sign):
        for direction, hops in ((sign, size // 2), (-sign, size // 2 - 1)):
            at = start
            for _ in range(hops):
                step = (direction, 0) if axis == 0 else (0, direction)
                child = norm((at[0] + step[0], at[1] + step[1]))
                parent[child] = (at, step)
                at = child

    root = (0, 0)
    if part == 0:
        ring(root, 1, NY, 1)
        for ny in range(NY):
            ring((0, ny), 0, NZ, 1 if ny % 2 == 0 else -1)
    else:
        ring(root, 0, NZ, -1)
        for nz in range(NZ):
            ring((nz, 0), 1, NY, -1 if nz % 2 == 0 else 1)
    return parent


TREES = (make_tree(0), make_tree(1))
CHILDREN = []
DEPTH = []
HEIGHT = []
for tree in TREES:
    kids = {}
    for child, (par, step) in tree.items():
        kids.setdefault(par, []).append((child, step))
    depth = {(0, 0): 0}
    todo = [(0, 0)]
    order = []
    while todo:
        at = todo.pop(0)
        order.append(at)
        for child, _ in kids.get(at, []):
            depth[child] = depth[at] + 1
            todo.append(child)
    height = {}
    for at in reversed(order):
        height[at] = max([1 + height[c] for c, _ in kids.get(at, [])], default=0)
    for at in kids:
        kids[at].sort(key=lambda item: -height[item[0]])
    CHILDREN.append(kids)
    DEPTH.append(depth)
    HEIGHT.append(height)

EDGES = [(p, n) for p in (0, 1) for n in sorted(TREES[p])]
EDGE_ID = {edge: i for i, edge in enumerate(EDGES)}
LINK_US = [rows * CH * 2 * 2 / 90e3 for _, rows in ROWS]
HOP_US = 1.7


def plan_gather():
    free, arrivals, events = {}, [], []
    state = {"t": 0.0}

    def forward(p, n):
        for child, step in CHILDREN[p].get(n, []):
            begin = max(state["t"], free.get(step, 0.0))
            free[step] = begin + LINK_US[p]
            heapq.heappush(arrivals, (free[step] + HOP_US, p, child))

    for p in (1, 0):
        forward(p, (0, 0))
    seen = {}
    ready = [(0, 0)]
    done = 0
    while arrivals or ready:
        if arrivals and arrivals[0][0] <= state["t"]:
            _, p, n = heapq.heappop(arrivals)
            events.append(("recv", p, n))
            state["t"] += 0.05
            forward(p, n)
            seen[n] = seen.get(n, 0) + 1
            if seen[n] == 2:
                ready.append(n)
        elif ready:
            n = ready.pop(0)
            events.append(("comp", n))
            state["t"] += 0.45
            done += 1
        else:
            state["t"] = arrivals[0][0]
    return events, state["t"]


def plan_reduce():
    free, arrivals, order = {}, [], []
    t = 0.0
    missing = {(p, n): len(CHILDREN[p].get(n, [])) for p in (0, 1) for n in list(TREES[p]) + [(0, 0)]}
    ready = [key for key, count in missing.items() if count == 0]
    while arrivals or ready:
        while arrivals and arrivals[0][0] <= t:
            _, p, n = heapq.heappop(arrivals)
            missing[(p, n)] -= 1
            if missing[(p, n)] == 0:
                ready.append((p, n))

        def key(item):
            p, n = item
            if n == (0, 0):
                return (2, 0.0)
            backlog = free.get(TREES[p][n][1], 0.0) - t
            return (0 if backlog < 2.5 else 1, -DEPTH[p][n], backlog)

        ready.sort(key=key)
        if ready and (key(ready[0])[0] == 0 or not arrivals or key(ready[0])[0] == 2):
            p, n = ready.pop(0)
            order.append((p, n))
            t += 0.3
            if n != (0, 0):
                par, step = TREES[p][n]
                begin = max(t, free.get(step, 0.0))
                free[step] = begin + LINK_US[p]
                heapq.heappush(arrivals, (free[step] + HOP_US, p, par))
        else:
            nexts = [arrivals[0][0]] if arrivals else []
            if ready:
                nexts.append(t + 0.2)
            t = min(nexts)
    return order, t


GATHER, GATHER_US = plan_gather()
REDUCE, REDUCE_US = plan_reduce()


def rope_table(length):
    half = HD // 2
    inverse = np.exp(np.arange(half) * (-2.0 * math.log(rope_base) / HD))
    angles = np.arange(length)[:, None] * inverse[None, :]
    return np.concatenate([np.cos(angles), np.sin(angles)], axis=1).astype(np.float32)


def dot(a, b):
    return jnp.dot(a, b, preferred_element_type=F32)


def dot_nt(a, b, precision=None):
    return lax.dot_general(a, b, (((1,), (1,)), ((), ())), preferred_element_type=F32, precision=precision)


def kernel(
    act, gain, wq_h, kv_h, wo_h, ids, clean, rope_h, out,
    xg, held, wq, kvraw, wo, rope, perm, acc_m, acc_o, orecv, qbuf, kv, num, den, att, sbuf, rbuf,
    sqz, sqy, sqs,
    g_send, g_recv, r_send, r_recv, s_send, s_recv, x_send, x_recv, c_send, c_recv, load_sem,
):
    col = lax.axis_index("col")
    row = lax.axis_index("row")
    seq = lax.axis_index("seq")
    z, y = col // NY, lax.rem(col, NY)
    other = 1 - row

    def plane(step):
        zz = lax.rem(z + step[0] + NZ, NZ)
        yy = lax.rem(y + step[1] + NY, NY)
        return {"col": zz * NY + yy}

    def origin(n):
        return lax.rem(z + NZ - n[0] % NZ, NZ) * NY + lax.rem(y + NY - n[1] % NY, NY)

    def along(step):
        return {"seq": lax.rem(seq + step + 4, 4)}

    sibling = {"row": other}

    barrier = pltpu.get_barrier_semaphore()
    partners = [plane(s) for s in ((1, 0), (-1, 0), (0, 1), (0, -1))] + [along(1), along(-1), sibling]
    for device in partners:
        pl.semaphore_signal(barrier, inc=1, device_id=device, device_id_type=MESH)

    def dyn(index, size):
        return pl.ds(pl.multiple_of(index * size, size), size)

    group = col // 8
    loads = [
        pltpu.make_async_copy(wq_h.at[:, dyn(row, HD)], wq.at[:, pl.ds(0, HD)], load_sem.at[0]),
        pltpu.make_async_copy(wq_h.at[:, dyn(other, HD)], wq.at[:, pl.ds(HD, HD)], load_sem.at[1]),
        pltpu.make_async_copy(kv_h.at[:, :, dyn(group, HD)], kvraw, load_sem.at[2]),
        pltpu.make_async_copy(rope_h.at[dyn(seq, SLAB), :], rope, load_sem.at[3]),
        pltpu.make_async_copy(wo_h.at[dyn(row, HD), :], wo.at[pl.ds(0, HD), :], load_sem.at[4]),
        pltpu.make_async_copy(wo_h.at[dyn(other, HD), :], wo.at[pl.ds(HD, HD), :], load_sem.at[5]),
    ]
    for copy in loads:
        copy.start()

    wide = act[...].astype(F32)
    xg[...] = (wide * gain[...]).astype(BF16)
    pl.semaphore_wait(barrier, len(partners))

    sent = []

    def remote(src, dst, send, recv, device):
        return pltpu.make_async_remote_copy(
            src_ref=src, dst_ref=dst, send_sem=send, recv_sem=recv, device_id=device, device_id_type=MESH
        )

    def launch(copy):
        copy.start()
        sent.append(copy)

    def chunk(n, p):
        first, rows = ROWS[p]
        if n == (0, 0):
            return xg.at[pl.ds(first, rows), :]
        return held.at[slot(n), pl.ds(first, rows), :]

    def gather_copy(p, n, child, step):
        e = EDGE_ID[(p, child)]
        return remote(chunk(n, p), chunk(child, p), g_send.at[e], g_recv.at[e], plane(step))

    def forward(p, n):
        for child, step in CHILDREN[p].get(n, []):
            launch(gather_copy(p, n, child, step))

    forward(1, (0, 0))
    forward(0, (0, 0))

    ones = jnp.ones((8, CH), F32)
    sqz[0] = dot_nt(ones, wide * wide, lax.Precision.HIGHEST)

    def sqz_forward(nz):
        for child, step in CHILDREN[1].get((nz, 0), []):
            if step[0]:
                k = child[0]
                launch(remote(sqz.at[nz], sqz.at[k], s_send.at[k], s_recv.at[k], plane(step)))

    def sqy_forward(ny):
        for child, step in CHILDREN[0].get((0, ny), []):
            if step[1]:
                k = child[1]
                launch(remote(sqy.at[ny], sqy.at[k], s_send.at[8 + k], s_recv.at[8 + k], plane(step)))

    def landed(dst, recv, device):
        remote(dst, dst, recv, recv, device).wait_recv()

    sqz_forward(0)

    line = lax.broadcasted_iota(jnp.int32, (2 * CH, 2 * CH), 0)
    lane = lax.broadcasted_iota(jnp.int32, (2 * CH, 2 * CH), 1)
    upper = (line >= CH).astype(jnp.int32)
    kind = jnp.where(row == 0, upper, 1 - upper)
    perm[...] = jnp.where(lane == 2 * (line - CH * upper) + kind, 1.0, 0.0).astype(BF16)
    acc_m[...] = jnp.zeros_like(acc_m)
    acc_o[...] = jnp.zeros_like(acc_o)
    for copy in loads[:4]:
        copy.wait()

    def compute(n):
        at = origin(n)
        wrow = dyn(at, CH)
        pairs = kvraw[wrow, :, :].reshape(2 * CH, HD)
        split = dot(perm[...], pairs).astype(BF16)
        mine = jnp.concatenate([wq[wrow, pl.ds(0, HD)], split[:CH]], axis=1)
        theirs = jnp.concatenate([wq[wrow, pl.ds(HD, HD)], split[CH:]], axis=1)
        x = xg[...] if n == (0, 0) else held[slot(n)]
        acc_m[...] += dot(x, mine)
        acc_o[...] += dot(x, theirs)

    z_left = NZ - 1
    events = list(GATHER)
    for position, event in enumerate(events):
        if event[0] == "comp":
            compute(event[1])
            continue
        _, p, n = event
        step = TREES[p][n][1]
        e = EDGE_ID[(p, n)]
        landed(chunk(n, p), g_recv.at[e], plane((-step[0], -step[1])))
        forward(p, n)
        if p == 1 and n[1] == 0:
            landed(sqz.at[n[0]], s_recv.at[n[0]], plane((-step[0], -step[1])))
            sqz_forward(n[0])
            z_left -= 1
            if z_left == 0:
                total = sqz[0]
                for k in range(1, NZ):
                    total = total + sqz[k]
                sqy[0] = total
                sqy_forward(0)
        if position == len(events) - 16:
            landed(sqy.at[1], s_recv.at[9], plane((0, -1)))
            sqy_forward(1)
        if position == len(events) - 4:
            pass

    launch(remote(acc_o, orecv, c_send.at[0], c_recv.at[0], sibling))
    landed(sqy.at[2], s_recv.at[10], plane((0, -1)))
    landed(sqy.at[3], s_recv.at[11], plane((0, 1)))
    sqs[0] = sqy[0] + sqy[1] + sqy[2] + sqy[3]
    launch(remote(sqs.at[0], sqs.at[1], c_send.at[1], c_recv.at[1], sibling))

    table = rope[...]
    turned = pltpu.roll(table, HD // 2, 1)
    low = lax.broadcasted_iota(jnp.int32, (SLAB, HD), 1) < HD // 2
    cosine = jnp.where(low, table, turned)
    sine = jnp.where(low, -turned, table)
    is_key = (row == 0).astype(F32)
    cos_kv = cosine * is_key + (1.0 - is_key)
    sin_kv = sine * is_key

    landed(sqs.at[1], c_recv.at[1], sibling)
    squares = sqs[0] + sqs[1]
    scaling = lax.rsqrt(squares[:1] / D + norm_eps)
    scale_col = jnp.broadcast_to(scaling, (HD, SLAB)).T
    my_ids = ids[:, dyn(seq, SLAB)].astype(F32)
    own = jnp.broadcast_to(my_ids, (HD, SLAB)).T

    landed(orecv, c_recv.at[0], sibling)
    kv_sum = (acc_m[:, HD:] + orecv[:, HD:]) * scale_col
    kv[row, 0] = (kv_sum * cos_kv + pltpu.roll(kv_sum, HD // 2, 1) * sin_kv).astype(BF16)

    half = SLAB // 2
    launch(remote(kv.at[row, 0], kv.at[row, 1], x_send.at[0], x_recv.at[0], along(1)))
    launch(remote(kv.at[row, 0], kv.at[row, 3], x_send.at[1], x_recv.at[1], along(-1)))
    launch(remote(kv.at[row, 0], kv.at[row, 0], c_send.at[2], c_recv.at[2], sibling))

    q_sum = (acc_m[:, :HD] + orecv[:, :HD]) * scale_col
    qbuf[...] = (q_sum * cosine + pltpu.roll(q_sum, HD // 2, 1) * sine).astype(BF16)
    num[...] = jnp.zeros_like(num)
    den[...] = jnp.zeros_like(den)
    score_scale = 1.0 / math.sqrt(HD)

    own_ids = own

    def attend(k):
        from_seq = lax.rem(seq + 4 - k, 4)
        key_ids = ids[:, dyn(from_seq, SLAB)].astype(F32)
        open_to = jnp.where(clean[:, dyn(from_seq, SLAB)] == 1, 1e9, key_ids)
        scores = dot_nt(qbuf[...], kv[0, k]) * score_scale
        mine = own_ids[:, :1]
        visible = (mine >= key_ids) & (mine <= open_to)
        weights = jnp.where(visible, jnp.exp(scores), 0.0)
        den[...] += weights[:, 0:128] + weights[:, 128:256] + weights[:, 256:384] + weights[:, 384:512]
        num[...] += dot(weights.astype(BF16), kv[1, k])

    landed(kv.at[other, 0], c_recv.at[2], sibling)
    landed(kv.at[row, 1], x_recv.at[0], along(-1))
    launch(remote(kv.at[row, 1, pl.ds(0, half)], kv.at[row, 2, pl.ds(0, half)], x_send.at[2], x_recv.at[2], along(1)))
    launch(remote(kv.at[row, 1], kv.at[row, 1], c_send.at[3], c_recv.at[3], sibling))
    landed(kv.at[row, 3], x_recv.at[1], along(1))
    launch(
        remote(kv.at[row, 3, pl.ds(half, half)], kv.at[row, 2, pl.ds(half, half)], x_send.at[3], x_recv.at[3], along(-1))
    )
    launch(remote(kv.at[row, 3], kv.at[row, 3], c_send.at[4], c_recv.at[4], sibling))
    attend(0)
    landed(kv.at[row, 2, pl.ds(0, half)], x_recv.at[2], along(-1))
    landed(kv.at[row, 2, pl.ds(half, half)], x_recv.at[3], along(1))
    launch(remote(kv.at[row, 2], kv.at[row, 2], c_send.at[5], c_recv.at[5], sibling))
    landed(kv.at[other, 1], c_recv.at[3], sibling)
    attend(1)
    landed(kv.at[other, 3], c_recv.at[4], sibling)
    attend(3)
    landed(kv.at[other, 2], c_recv.at[5], sibling)
    attend(2)

    att[0] = (num[...] / jnp.sum(den[...], axis=1, keepdims=True)).astype(BF16)
    launch(remote(att.at[0], att.at[1], c_send.at[6], c_recv.at[6], sibling))
    for copy in loads[4:]:
        copy.wait()
    landed(att.at[1], c_recv.at[6], sibling)

    for p, n in REDUCE:
        first, rows = ROWS[p]
        block = pl.ds(first, rows)
        left = jnp.concatenate([att[0, block, :], att[1, block, :]], axis=1)
        value = dot(left, wo[:, dyn(origin(n), CH)])
        for child, step in CHILDREN[p].get(n, []):
            e = EDGE_ID[(p, child)]
            landed(rbuf.at[slot(child), block, :], r_recv.at[e], plane(step))
            value = value + rbuf[slot(child), block, :].astype(F32)
        if n == (0, 0):
            out[block, :] = value.astype(BF16)
            continue
        e = EDGE_ID[(p, n)]
        step = TREES[p][n][1]
        sbuf[slot(n), block, :] = value.astype(BF16)
        launch(
            remote(
                sbuf.at[slot(n), block, :], rbuf.at[slot(n), block, :],
                r_send.at[e], r_recv.at[e], plane((-step[0], -step[1])),
            )
        )

    for copy in sent:
        copy.wait_send()


def shards(activations, norm_gain, query_weight, kv_weight, out_weight, block_ids, clean_mask):
    features = query_weight.shape[0]
    length = block_ids.shape[0]
    vmem = pl.BlockSpec(memory_space=pltpu.VMEM)
    hbm = pl.BlockSpec(memory_space=pl.ANY)
    dma = pltpu.SemaphoreType.DMA
    edges = len(EDGES)
    return pl.pallas_call(
        kernel,
        out_shape=jax.ShapeDtypeStruct((SLAB, CH), BF16),
        in_specs=[vmem, vmem, hbm, hbm, hbm, vmem, vmem, hbm],
        out_specs=vmem,
        scratch_shapes=[
            pltpu.VMEM((SLAB, CH), BF16),
            pltpu.VMEM((NZ * NY, SLAB, CH), BF16),
            pltpu.VMEM((features, 2 * HD), BF16),
            pltpu.VMEM((features, 2, HD), BF16),
            pltpu.VMEM((2 * HD, out_weight.shape[1]), BF16),
            pltpu.VMEM((SLAB, HD), F32),
            pltpu.VMEM((2 * CH, 2 * CH), BF16),
            pltpu.VMEM((SLAB, 2 * HD), F32),
            pltpu.VMEM((SLAB, 2 * HD), F32),
            pltpu.VMEM((SLAB, 2 * HD), F32),
            pltpu.VMEM((SLAB, HD), BF16),
            pltpu.VMEM((2, 4, SLAB, HD), BF16),
            pltpu.VMEM((SLAB, HD), F32),
            pltpu.VMEM((SLAB, HD), F32),
            pltpu.VMEM((2, SLAB, HD), BF16),
            pltpu.VMEM((NZ * NY, SLAB, CH), BF16),
            pltpu.VMEM((NZ * NY, SLAB, CH), BF16),
            pltpu.VMEM((NZ, 8, SLAB), F32),
            pltpu.VMEM((NY, 8, SLAB), F32),
            pltpu.VMEM((2, 8, SLAB), F32),
            dma((edges,)), dma((edges,)), dma((edges,)), dma((edges,)),
            dma((12,)), dma((12,)), dma((4,)), dma((4,)), dma((7,)), dma((7,)), dma((6,)),
        ],
        compiler_params=pltpu.CompilerParams(
            collective_id=0, has_side_effects=True, vmem_limit_bytes=63 * 1024 * 1024
        ),
        name="layer",
    )(
        activations,
        norm_gain.reshape(1, CH),
        query_weight,
        kv_weight,
        out_weight,
        block_ids.reshape(1, length),
        clean_mask.reshape(1, length),
        jnp.asarray(rope_table(length)),
    )


def solution(mesh):
    placed = (
        P("seq", ("row", "col")),
        P(("row", "col")),
        P("row", "col"),
        P("row", None, None),
        P("col", "row"),
        P(),
        P(),
    )
    return jax.shard_map(
        shards, mesh=mesh, in_specs=placed, out_specs=P("seq", ("row", "col")), check_vma=False
    )
```

```python
import heapq
import math
import random

import jax
import jax.numpy as jnp
import numpy as np
from jax import lax
from jax.experimental import pallas as pl
from jax.experimental.pallas import tpu as pltpu
from jax.sharding import PartitionSpec as P

D = 16384
HD = 128
QH = 64
KVH = 4
rope_base = 500000.0
norm_eps = 1e-05

MESH = pl.DeviceIdType.MESH
VMEM_LIMIT = 63 * 1024 * 1024
F32 = jnp.float32
BF16 = jnp.bfloat16

NZ, NY = 8, 4
SLAB = 512
SPLIT = 208
PARTS = ((0, SPLIT, True), (SPLIT, SLAB - SPLIT, False))
ROWS = tuple(part[:2] for part in PARTS)
CH = 256


def norm(n):
    return (n[0] % NZ, n[1] % NY)


def slot(n):
    return (n[0] % NZ) * NY + n[1] % NY


HOP_US = 1.7
COMP_US = 0.3
LOADED_US = 8.0
HALVED = True

HALVES = tuple(
    (slice(first, first + (rows // 32 + rows % 32 // 16) * 16), slice(first + (rows // 32 + rows % 32 // 16) * 16, first + rows))
    for first, rows in ROWS
)
WHOLE = tuple(slice(first, first + rows) for first, rows in ROWS)


def make_tree(part, y_first):
    edges = []

    def ring(start, axis, size, way, halved):
        for direction, hops in ((way, size // 2), (-way, size // 2 - 1)):
            at = start
            for hop in range(1, size // 2 + 1):
                step = (direction, 0) if axis == 0 else (0, direction)
                child = norm((at[0] + step[0], at[1] + step[1]))
                far = hop == size // 2
                if far and halved:
                    edges.append((at, child, step, HALVES[part][direction == way]))
                elif hop <= hops:
                    edges.append((at, child, step, WHOLE[part]))
                at = child

    root = (0, 0)
    if y_first:
        ring(root, 1, NY, 1, HALVED)
        for ny in range(NY):
            ring((0, ny), 0, NZ, 1 if ny % 2 == 0 else -1, False)
    else:
        ring(root, 0, NZ, -1, HALVED)
        for nz in range(NZ):
            ring((nz, 0), 1, NY, -1 if nz % 2 == 0 else 1, False)
    return edges


EDGES = [(part,) + edge for part, spec in enumerate(PARTS) for edge in make_tree(part, spec[2])]
DOWN, UP = {}, {}
for number, edge in enumerate(EDGES):
    DOWN.setdefault((edge[0], edge[1]), []).append(number)
    UP.setdefault((edge[0], edge[2]), []).append(number)
NODES = [(part, (nz, ny)) for part in range(len(PARTS)) for nz in range(NZ) for ny in range(NY)]


def height(key):
    return max([1 + height((key[0], EDGES[e][2])) for e in DOWN.get(key, [])], default=0)


def depth(key):
    return max([1 + depth((key[0], EDGES[e][1])) for e in UP.get(key, [])], default=0)


DEPTH = {key: depth(key) for key in NODES}
for key in DOWN:
    DOWN[key].sort(key=lambda e: -height((EDGES[e][0], EDGES[e][2])))


def link_us(e):
    rows = EDGES[e][4]
    return (rows.stop - rows.start) * CH * 2 * 2 / 95e3


def tail_down(key):
    return max([link_us(e) + HOP_US + tail_down((key[0], EDGES[e][2])) for e in DOWN.get(key, [])], default=0.0)


def tail_up(key):
    return max([link_us(e) + HOP_US + 0.3 + tail_up((key[0], EDGES[e][1])) for e in UP.get(key, [])], default=0.0)


def plan_gather(backlog=1.0):
    rank = [tail_down((edge[0], edge[2])) for edge in EDGES]
    free, arrivals, events = {}, [], []
    pending = [e for part in (0, 1) for e in DOWN[(part, (0, 0))]]
    missing = {key: len(UP.get(key, [])) for key in NODES}
    ready = [(0, (0, 0)), (1, (0, 0))]
    t = 0.0
    while arrivals or ready or pending:
        able = [e for e in pending if free.get(EDGES[e][3], 0.0) - t < backlog]
        if able:
            e = max(able, key=lambda e: rank[e])
            pending.remove(e)
            step = EDGES[e][3]
            free[step] = max(t, free.get(step, 0.0)) + link_us(e)
            heapq.heappush(arrivals, (free[step] + HOP_US, e))
            events.append(("send", e))
            t += 0.01
        elif arrivals and arrivals[0][0] <= t:
            _, e = heapq.heappop(arrivals)
            events.append(("recv", e))
            t += 0.04
            key = (EDGES[e][0], EDGES[e][2])
            missing[key] -= 1
            if missing[key] == 0:
                pending += DOWN.get(key, [])
                ready.append(key)
        elif ready and t >= LOADED_US:
            events.append(("comp",) + ready.pop(0))
            t += COMP_US
        else:
            nexts = [arrivals[0][0]] if arrivals else []
            if t < LOADED_US:
                nexts.append(LOADED_US)
            if pending:
                nexts.append(min(free[EDGES[e][3]] for e in pending) - backlog + 0.001)
            t = max(t + 0.001, min(nexts))
    return events, t


def plan_reduce(backlog=2.0, jitter=0.5, seed=1):
    draw = random.Random(seed)
    rank = {key: tail_up(key) + jitter * draw.random() for key in NODES}
    free, arrivals, order = {}, [], []
    missing = {key: len(DOWN.get(key, [])) for key in NODES}
    ready = [key for key in NODES if missing[key] == 0]
    t = 0.0

    def behind(key):
        return max(free.get(EDGES[e][3], 0.0) for e in UP[key]) - t

    while arrivals or ready:
        while arrivals and arrivals[0][0] <= t:
            _, e = heapq.heappop(arrivals)
            above = (EDGES[e][0], EDGES[e][1])
            missing[above] -= 1
            if missing[above] == 0:
                ready.append(above)
        able = [key for key in ready if key in UP and behind(key) < backlog]
        roots = [key for key in ready if key not in UP]
        if able:
            key = max(able, key=lambda key: rank[key] - 0.5 * max(0.0, behind(key)))
        elif roots:
            key = roots[0]
        else:
            nexts = [arrivals[0][0]] if arrivals else []
            if ready:
                nexts.append(min(behind(key) for key in ready) + t - backlog + 0.001)
            t = max(t + 0.001, min(nexts))
            continue
        ready.remove(key)
        order.append(key)
        t += 0.1 + 0.2 * ROWS[key[0]][1] / CH
        for e in UP.get(key, []):
            step = EDGES[e][3]
            free[step] = max(t, free.get(step, 0.0)) + link_us(e)
            heapq.heappush(arrivals, (free[step] + HOP_US, e))
    return order, t


GATHER, GATHER_US = plan_gather()
REDUCE, REDUCE_US = plan_reduce()
RECVS = [i for i, event in enumerate(GATHER) if event[0] == "recv"]
FIRST_AT, SQUARES_AT = RECVS[4], (RECVS[-18], RECVS[-11], RECVS[-5])


def rope_tables():
    half = HD // 2
    inverse = np.exp(np.arange(half) * (-2.0 * math.log(rope_base) / HD))
    angles = np.arange(SLAB)[:, None] * inverse[None, :]
    within = np.concatenate([np.cos(angles), np.sin(angles)], axis=1)
    starts = np.tile(np.arange(4)[:, None] * SLAB * inverse[None, :], (1, 2))
    return within.astype(np.float32), np.concatenate([np.cos(starts), np.sin(starts)]).astype(np.float32)


def dot(a, b):
    return jnp.dot(a, b, preferred_element_type=F32)


def dot_nt(a, b, precision=None):
    return lax.dot_general(a, b, (((1,), (1,)), ((), ())), preferred_element_type=F32, precision=precision)


def kernel(
    act_h, gain_h, wq_h, kv_h, wo_h, ids_h, clean_h, within_h, starts_h, out,
    act, gain, ids, clean, within, starts,
    xg, held, wq, kvraw, wkv, wo, perm, cosine, sine, scale_col, own_ids,
    accq_m, acckv_m, accq_o, acckv_o, recvq, recvkv, qbuf, kv, num, den, att, sbuf, rbuf,
    sqz, sqy, sqs,
    g_send, g_recv, r_send, r_recv, s_send, s_recv, x_send, x_recv, c_send, c_recv, load_sem,
):
    col = lax.axis_index("col")
    row = lax.axis_index("row")
    seq = lax.axis_index("seq")
    z, y = col // NY, lax.rem(col, NY)
    other = 1 - row

    def plane(step):
        zz = lax.rem(z + step[0] + NZ, NZ)
        yy = lax.rem(y + step[1] + NY, NY)
        return {"col": zz * NY + yy}

    def origin(n):
        return lax.rem(z + NZ - n[0] % NZ, NZ) * NY + lax.rem(y + NY - n[1] % NY, NY)

    def along(step):
        return {"seq": lax.rem(seq + step + 4, 4)}

    sibling = {"row": other}

    barrier = pltpu.get_barrier_semaphore()
    partners = [plane(s) for s in ((1, 0), (-1, 0), (0, 1), (0, -1))] + [along(1), along(-1), sibling]
    for device in partners:
        pl.semaphore_signal(barrier, inc=1, device_id=device, device_id_type=MESH)

    def dyn(index, size):
        return pl.ds(pl.multiple_of(index * size, size), size)

    group = col // 8
    pieces = (
        (act_h, act),
        (gain_h, gain),
        (kv_h.at[:, :, dyn(group, HD)], kvraw),
        (wq_h.at[:, dyn(row, HD)], wq.at[:, pl.ds(0, HD)]),
        (wq_h.at[:, dyn(other, HD)], wq.at[:, pl.ds(HD, HD)]),
        (within_h, within),
        (starts_h, starts),
        (ids_h, ids),
        (clean_h, clean),
        (wo_h.at[dyn(row, HD), :], wo.at[pl.ds(0, HD), :]),
        (wo_h.at[dyn(other, HD), :], wo.at[pl.ds(HD, HD), :]),
    )
    loads = [pltpu.make_async_copy(src, dst, load_sem.at[i]) for i, (src, dst) in enumerate(pieces)]
    for copy in loads:
        copy.start()
    loads[0].wait()
    loads[1].wait()
    wide = act[...].astype(F32)
    xg[...] = (wide * gain[...]).astype(BF16)
    pl.semaphore_wait(barrier, len(partners))

    sent = []

    def remote(src, dst, send, recv, device):
        return pltpu.make_async_remote_copy(
            src_ref=src, dst_ref=dst, send_sem=send, recv_sem=recv, device_id=device, device_id_type=MESH
        )

    def launch(copy):
        copy.start()
        sent.append(copy)

    def landed(dst, recv, device):
        remote(dst, dst, recv, recv, device).wait_recv()

    def chunk(n, rows):
        block = pl.ds(rows.start, rows.stop - rows.start)
        if n == (0, 0):
            return xg.at[block, :]
        return held.at[slot(n), block, :]

    def send(e):
        _, above, below, step, rows = EDGES[e]
        launch(remote(chunk(above, rows), chunk(below, rows), g_send.at[e], g_recv.at[e], plane(step)))

    own_sends = next(i for i, event in enumerate(GATHER) if event[0] != "send")
    for event in GATHER[:own_sends]:
        send(event[1])

    sqz[0] = dot_nt(jnp.ones((8, CH), F32), wide * wide, lax.Precision.HIGHEST)

    def square_ring(ref, at, axis, base):
        size = ref.shape[0]
        for direction, hops in ((1, size // 2), (-1, size // 2 - 1)):
            distance = at if direction == 1 else (size - at) % size
            if distance < hops and (at == 0 or distance < size // 2):
                k = (at + direction) % size
                step = (direction, 0) if axis == 0 else (0, direction)
                launch(remote(ref.at[at], ref.at[k], s_send.at[base + k], s_recv.at[base + k], plane(step)))

    def sqz_forward(nz):
        square_ring(sqz, nz, 0, 0)

    def sqy_forward(ny):
        square_ring(sqy, ny, 1, 8)

    sqz_forward(0)

    line = lax.broadcasted_iota(jnp.int32, (2 * CH, 2 * CH), 0)
    lane = lax.broadcasted_iota(jnp.int32, (2 * CH, 2 * CH), 1)
    upper = (line >= CH).astype(jnp.int32)
    kind = jnp.where(row == 0, upper, 1 - upper)
    perm[...] = jnp.where(lane == 2 * (line - CH * upper) + kind, 1.0, 0.0).astype(BF16)
    for acc in (accq_m, acckv_m, accq_o, acckv_o):
        acc[...] = jnp.zeros_like(acc)

    apart = set()

    def compute(pair, n):
        if not apart:
            for copy in loads[2:5]:
                copy.wait()
        at = dyn(origin(n), CH)
        if n not in apart:
            apart.add(n)
            split = dot(perm[...], kvraw[at, :, :].reshape(2 * CH, HD)).astype(BF16)
            wkv[at, pl.ds(0, HD)] = split[:CH]
            wkv[at, pl.ds(HD, HD)] = split[CH:]
        first, rows = ROWS[pair]
        block = pl.ds(first, rows)
        x = xg[block, :] if n == (0, 0) else held[slot(n), block, :]
        theirs = dot(x, jnp.concatenate([wkv[at, pl.ds(HD, HD)], wq[at, pl.ds(HD, HD)]], axis=1))
        acckv_o[block, :] += theirs[:, :HD]
        accq_o[block, :] += theirs[:, HD:]
        mine = dot(x, jnp.concatenate([wkv[at, pl.ds(0, HD)], wq[at, pl.ds(0, HD)]], axis=1))
        acckv_m[block, :] += mine[:, :HD]
        accq_m[block, :] += mine[:, HD:]

    def prepare():
        for copy in loads[5:9]:
            copy.wait()
        table = within[...]
        turned = pltpu.roll(table, HD // 2, 1)
        low = lax.broadcasted_iota(jnp.int32, (SLAB, HD), 1) < HD // 2
        cos_t, sin_t = jnp.where(low, table, turned), jnp.where(low, turned, table)
        cos_s, sin_s = starts[pl.ds(seq, 1), :], starts[pl.ds(seq + 4, 1), :]
        cosine[...] = cos_t * cos_s - sin_t * sin_s
        both = sin_t * cos_s + cos_t * sin_s
        sine[...] = jnp.where(low, -both, both)
        own_ids[...] = jnp.broadcast_to(ids[:, dyn(seq, SLAB)].astype(F32), (HD, SLAB)).T
        num[...] = jnp.zeros_like(num)
        den[...] = jnp.zeros_like(den)

    z_left = NZ - 1
    missing = {key: len(UP.get(key, [])) for key in NODES}
    for position, event in enumerate(GATHER):
        if position < own_sends:
            continue
        if position == FIRST_AT:
            prepare()
        if position == SQUARES_AT[0]:
            landed(sqy.at[1], s_recv.at[9], plane((0, -1)))
            sqy_forward(1)
        if position == SQUARES_AT[1]:
            landed(sqy.at[2], s_recv.at[10], plane((0, -1)))
            landed(sqy.at[3], s_recv.at[11], plane((0, 1)))
            sqs[0] = sqy[0] + sqy[1] + sqy[2] + sqy[3]
            launch(remote(sqs.at[0], sqs.at[1], c_send.at[1], c_recv.at[1], sibling))
        if position == SQUARES_AT[2]:
            landed(sqs.at[1], c_recv.at[1], sibling)
            squares = sqs[0] + sqs[1]
            scaling = lax.rsqrt(squares[:1] / D + norm_eps)
            scale_col[...] = jnp.broadcast_to(scaling, (HD, SLAB)).T
        if event[0] == "comp":
            compute(event[1], event[2])
            continue
        if event[0] == "send":
            send(event[1])
            continue
        part, above, n, step, rows = EDGES[event[1]]
        landed(chunk(n, rows), g_recv.at[event[1]], plane((-step[0], -step[1])))
        missing[(part, n)] -= 1
        if missing[(part, n)]:
            continue
        if part == 1 and n[1] == 0:
            landed(sqz.at[n[0]], s_recv.at[n[0]], plane((-1, 0) if n[0] <= NZ // 2 else (1, 0)))
            sqz_forward(n[0])
            z_left -= 1
            if z_left == 0:
                total = sqz[0]
                for k in range(1, NZ):
                    total = total + sqz[k]
                sqy[0] = total
                sqy_forward(0)

    launch(remote(acckv_o, recvkv, c_send.at[0], c_recv.at[0], sibling))
    launch(remote(accq_o, recvq, c_send.at[7], c_recv.at[7], sibling))

    half = SLAB // 2
    halves = (pl.ds(0, half), pl.ds(half, half))
    is_key = (row == 0).astype(F32)
    landed(recvkv, c_recv.at[0], sibling)
    kv_sum = (acckv_m[...] + recvkv[...]) * scale_col[...]
    cos_kv = cosine[...] * is_key + (1.0 - is_key)
    kv[row, 0] = (kv_sum * cos_kv + pltpu.roll(kv_sum, HD // 2, 1) * (sine[...] * is_key)).astype(BF16)

    def over(source, target, part, sem, step):
        piece = halves[part]
        launch(
            remote(kv.at[row, source, piece], kv.at[row, target, piece], x_send.at[sem], x_recv.at[sem], along(step))
        )

    def arrived(target, part, sem, step):
        landed(kv.at[row, target, halves[part]], x_recv.at[sem], along(-step))

    def across(target, sem):
        launch(remote(kv.at[row, target], kv.at[row, target], c_send.at[sem], c_recv.at[sem], sibling))

    over(0, 1, 0, 0, 1)
    over(0, 3, 1, 1, -1)
    over(0, 1, 1, 2, 1)
    over(0, 3, 0, 3, -1)
    across(0, 2)

    landed(recvq, c_recv.at[7], sibling)
    q_sum = (accq_m[...] + recvq[...]) * scale_col[...]
    qbuf[...] = (q_sum * cosine[...] + pltpu.roll(q_sum, HD // 2, 1) * sine[...]).astype(BF16)
    score_scale = 1.0 / math.sqrt(HD)

    def attend(k, part=None):
        size = SLAB if part is None else half
        keys = pl.ds(0, SLAB) if part is None else halves[part]
        from_seq = lax.rem(seq + 4 - k, 4)
        place = pl.ds(pl.multiple_of(from_seq * SLAB + (part or 0) * half, half), size)
        key_ids = ids[:, place].astype(F32)
        open_to = jnp.where(clean[:, place] == 1, 1e9, key_ids)
        scores = dot_nt(qbuf[...], kv[0, k, keys, :]) * score_scale
        mine = own_ids[:, :1]
        visible = (mine >= key_ids) & (mine <= open_to)
        weights = jnp.where(visible, jnp.exp(scores), 0.0)
        share = weights[:, :HD]
        for first in range(HD, size, HD):
            share = share + weights[:, first : first + HD]
        den[...] += share
        num[...] += dot(weights.astype(BF16), kv[1, k, keys, :])

    arrived(1, 0, 0, 1)
    over(1, 2, 0, 4, 1)
    arrived(3, 1, 1, -1)
    over(3, 2, 1, 5, -1)
    landed(kv.at[other, 0], c_recv.at[2], sibling)
    arrived(1, 1, 2, 1)
    across(1, 3)
    arrived(3, 0, 3, -1)
    across(3, 4)
    attend(0)
    landed(kv.at[other, 1], c_recv.at[3], sibling)
    attend(1)
    arrived(2, 0, 4, 1)
    arrived(2, 1, 5, -1)
    across(2, 5)
    landed(kv.at[other, 3], c_recv.at[4], sibling)
    attend(3)
    landed(kv.at[other, 2], c_recv.at[5], sibling)
    attend(2)

    att[0] = (num[...] / jnp.sum(den[...], axis=1, keepdims=True)).astype(BF16)
    launch(remote(att.at[0], att.at[1], c_send.at[6], c_recv.at[6], sibling))
    for copy in loads[9:]:
        copy.wait()
    landed(att.at[1], c_recv.at[6], sibling)

    for p, n in REDUCE:
        first, rows = ROWS[p]
        block = pl.ds(first, rows)
        left = jnp.concatenate([att[0, block, :], att[1, block, :]], axis=1)
        value = dot(left, wo[:, dyn(origin(n), CH)])
        for e in DOWN.get((p, n), []):
            _, _, below, step, part = EDGES[e]
            piece = pl.ds(part.start, part.stop - part.start)
            landed(rbuf.at[slot(below), piece, :], r_recv.at[e], plane(step))
            term = rbuf[slot(below), piece, :].astype(F32)
            if part == WHOLE[p]:
                value = value + term
            elif part.start == first:
                cut = part.stop - first
                value = jnp.concatenate([value[:cut] + term, value[cut:]], axis=0)
            else:
                cut = part.start - first
                value = jnp.concatenate([value[:cut], value[cut:] + term], axis=0)
        if n == (0, 0):
            out[block, :] = value.astype(BF16)
            continue
        sbuf[slot(n), block, :] = value.astype(BF16)
        for e in UP[(p, n)]:
            _, _, _, step, part = EDGES[e]
            piece = pl.ds(part.start, part.stop - part.start)
            launch(
                remote(
                    sbuf.at[slot(n), piece, :], rbuf.at[slot(n), piece, :],
                    r_send.at[e], r_recv.at[e], plane((-step[0], -step[1])),
                )
            )

    for copy in sent:
        copy.wait_send()


def shards(activations, norm_gain, query_weight, kv_weight, out_weight, block_ids, clean_mask):
    features = query_weight.shape[0]
    length = block_ids.shape[0]
    vmem = pl.BlockSpec(memory_space=pltpu.VMEM)
    hbm = pl.BlockSpec(memory_space=pl.ANY)
    dma = pltpu.SemaphoreType.DMA
    edges = len(EDGES)
    tokens_f32 = pltpu.VMEM((SLAB, HD), F32)
    within, starts = rope_tables()
    return pl.pallas_call(
        kernel,
        out_shape=jax.ShapeDtypeStruct((SLAB, CH), BF16),
        in_specs=[hbm] * 9,
        out_specs=vmem,
        scratch_shapes=[
            pltpu.VMEM((SLAB, CH), BF16),
            pltpu.VMEM((1, CH), F32),
            pltpu.VMEM((1, length), jnp.int32),
            pltpu.VMEM((1, length), jnp.int32),
            tokens_f32,
            pltpu.VMEM((8, HD), F32),
            pltpu.VMEM((SLAB, CH), BF16),
            pltpu.VMEM((NZ * NY, SLAB, CH), BF16),
            pltpu.VMEM((features, 2 * HD), BF16),
            pltpu.VMEM((features, 2, HD), BF16),
            pltpu.VMEM((features, 2 * HD), BF16),
            pltpu.VMEM((2 * HD, out_weight.shape[1]), BF16),
            pltpu.VMEM((2 * CH, 2 * CH), BF16),
            tokens_f32, tokens_f32, tokens_f32, tokens_f32,
            tokens_f32, tokens_f32, tokens_f32, tokens_f32,
            tokens_f32, tokens_f32,
            pltpu.VMEM((SLAB, HD), BF16),
            pltpu.VMEM((2, 4, SLAB, HD), BF16),
            tokens_f32, tokens_f32,
            pltpu.VMEM((2, SLAB, HD), BF16),
            pltpu.VMEM((NZ * NY, SLAB, CH), BF16),
            pltpu.VMEM((NZ * NY, SLAB, CH), BF16),
            pltpu.VMEM((NZ, 8, SLAB), F32),
            pltpu.VMEM((NY, 8, SLAB), F32),
            pltpu.VMEM((2, 8, SLAB), F32),
            dma((edges,)), dma((edges,)), dma((edges,)), dma((edges,)),
            dma((12,)), dma((12,)), dma((6,)), dma((6,)), dma((8,)), dma((8,)), dma((11,)),
        ],
        compiler_params=pltpu.CompilerParams(
            collective_id=0, has_side_effects=True, vmem_limit_bytes=VMEM_LIMIT
        ),
        name="layer",
    )(
        activations,
        norm_gain.reshape(1, CH),
        query_weight,
        kv_weight,
        out_weight,
        block_ids.reshape(1, length),
        clean_mask.reshape(1, length),
        jnp.asarray(within),
        jnp.asarray(starts),
    )


def solution(mesh):
    placed = (
        P("seq", ("row", "col")),
        P(("row", "col")),
        P("row", "col"),
        P("row", None, None),
        P("col", "row"),
        P(),
        P(),
    )
    return jax.shard_map(
        shards, mesh=mesh, in_specs=placed, out_specs=P("seq", ("row", "col")), check_vma=False
    )
```

```python
import heapq
import math
import random

import jax
import jax.numpy as jnp
import numpy as np
from jax import lax
from jax.experimental import pallas as pl
from jax.experimental.pallas import tpu as pltpu
from jax.sharding import PartitionSpec as P

D = 16384
HD = 128
QH = 64
KVH = 4
rope_base = 500000.0
norm_eps = 1e-05

MESH = pl.DeviceIdType.MESH
VMEM_LIMIT = 63 * 1024 * 1024
F32 = jnp.float32
BF16 = jnp.bfloat16

NZ, NY = 8, 4
SLAB = 512
SPLIT = 208
PARTS = ((0, SPLIT, True), (SPLIT, SLAB - SPLIT, False))
ROWS = tuple(part[:2] for part in PARTS)
CH = 256


def norm(n):
    return (n[0] % NZ, n[1] % NY)


def slot(n):
    return (n[0] % NZ) * NY + n[1] % NY


HOP_US = 1.5
COMP_US = 0.3
LOADED_US = 8.0
HALVED = True

HALVES = tuple(
    (slice(first, first + (rows // 32 + rows % 32 // 16) * 16), slice(first + (rows // 32 + rows % 32 // 16) * 16, first + rows))
    for first, rows in ROWS
)
WHOLE = tuple(slice(first, first + rows) for first, rows in ROWS)


def make_tree(part, y_first):
    edges = []

    def ring(start, axis, size, way, halved):
        for direction, hops in ((way, size // 2), (-way, size // 2 - 1)):
            at = start
            for hop in range(1, size // 2 + 1):
                step = (direction, 0) if axis == 0 else (0, direction)
                child = norm((at[0] + step[0], at[1] + step[1]))
                far = hop == size // 2
                if far and halved:
                    edges.append((at, child, step, HALVES[part][direction == way]))
                elif hop <= hops:
                    edges.append((at, child, step, WHOLE[part]))
                at = child

    root = (0, 0)
    if y_first:
        ring(root, 1, NY, 1, HALVED)
        for ny in range(NY):
            ring((0, ny), 0, NZ, 1 if ny % 2 == 0 else -1, False)
    else:
        ring(root, 0, NZ, -1, HALVED)
        for nz in range(NZ):
            ring((nz, 0), 1, NY, -1 if nz % 2 == 0 else 1, False)
    return edges


EDGES = [(part,) + edge for part, spec in enumerate(PARTS) for edge in make_tree(part, spec[2])]
DOWN, UP = {}, {}
for number, edge in enumerate(EDGES):
    DOWN.setdefault((edge[0], edge[1]), []).append(number)
    UP.setdefault((edge[0], edge[2]), []).append(number)
NODES = [(part, (nz, ny)) for part in range(len(PARTS)) for nz in range(NZ) for ny in range(NY)]


def height(key):
    return max([1 + height((key[0], EDGES[e][2])) for e in DOWN.get(key, [])], default=0)


def depth(key):
    return max([1 + depth((key[0], EDGES[e][1])) for e in UP.get(key, [])], default=0)


DEPTH = {key: depth(key) for key in NODES}
for key in DOWN:
    DOWN[key].sort(key=lambda e: -height((EDGES[e][0], EDGES[e][2])))


def link_us(e):
    rows = EDGES[e][4]
    return (rows.stop - rows.start) * CH * 2 * 2 / 97e3


def tail_down(key):
    return max([link_us(e) + HOP_US + tail_down((key[0], EDGES[e][2])) for e in DOWN.get(key, [])], default=0.0)


def tail_up(key):
    return max([link_us(e) + HOP_US + 0.3 + tail_up((key[0], EDGES[e][1])) for e in UP.get(key, [])], default=0.0)


def plan_gather(backlog=1.0):
    rank = [tail_down((edge[0], edge[2])) for edge in EDGES]
    free, arrivals, events = {}, [], []
    pending = [e for part in (0, 1) for e in DOWN[(part, (0, 0))]]
    missing = {key: len(UP.get(key, [])) for key in NODES}
    ready = [(0, (0, 0)), (1, (0, 0))]
    t = 0.0
    while arrivals or ready or pending:
        able = [e for e in pending if free.get(EDGES[e][3], 0.0) - t < backlog]
        if able:
            e = max(able, key=lambda e: rank[e])
            pending.remove(e)
            step = EDGES[e][3]
            free[step] = max(t, free.get(step, 0.0)) + link_us(e)
            heapq.heappush(arrivals, (free[step] + HOP_US, e))
            events.append(("send", e))
            t += 0.01
        elif arrivals and arrivals[0][0] <= t:
            _, e = heapq.heappop(arrivals)
            events.append(("recv", e))
            t += 0.04
            key = (EDGES[e][0], EDGES[e][2])
            missing[key] -= 1
            if missing[key] == 0:
                pending += DOWN.get(key, [])
                ready.append(key)
        elif ready and t >= LOADED_US:
            events.append(("comp",) + ready.pop(0))
            t += COMP_US
        else:
            nexts = [arrivals[0][0]] if arrivals else []
            if t < LOADED_US:
                nexts.append(LOADED_US)
            if pending:
                nexts.append(min(free[EDGES[e][3]] for e in pending) - backlog + 0.001)
            t = max(t + 0.001, min(nexts))
    return events, t


def plan_reduce(backlog=2.0, jitter=0.5, seed=1):
    draw = random.Random(seed)
    rank = {key: tail_up(key) + jitter * draw.random() for key in NODES}
    free, arrivals, order = {}, [], []
    missing = {key: len(DOWN.get(key, [])) for key in NODES}
    ready = [key for key in NODES if missing[key] == 0]
    t = 0.0

    def behind(key):
        return max(free.get(EDGES[e][3], 0.0) for e in UP[key]) - t

    while arrivals or ready:
        while arrivals and arrivals[0][0] <= t:
            _, e = heapq.heappop(arrivals)
            above = (EDGES[e][0], EDGES[e][1])
            missing[above] -= 1
            if missing[above] == 0:
                ready.append(above)
        able = [key for key in ready if key in UP and behind(key) < backlog]
        roots = [key for key in ready if key not in UP]
        if able:
            key = max(able, key=lambda key: rank[key] - 0.5 * max(0.0, behind(key)))
        elif roots:
            key = roots[0]
        else:
            nexts = [arrivals[0][0]] if arrivals else []
            if ready:
                nexts.append(min(behind(key) for key in ready) + t - backlog + 0.001)
            t = max(t + 0.001, min(nexts))
            continue
        ready.remove(key)
        order.append(key)
        t += 0.1 + 0.2 * ROWS[key[0]][1] / CH
        for e in UP.get(key, []):
            step = EDGES[e][3]
            free[step] = max(t, free.get(step, 0.0)) + link_us(e)
            heapq.heappush(arrivals, (free[step] + HOP_US, e))
    return order, t


GATHER, GATHER_US = plan_gather()
REDUCE, REDUCE_US = plan_reduce()
LAST_COMP = [max(i for i, event in enumerate(GATHER) if event[:2] == ("comp", part)) for part in (0, 1)]
RECVS = [i for i, event in enumerate(GATHER) if event[0] == "recv"]
FIRST_AT, SQUARES_AT = RECVS[4], (RECVS[-18], RECVS[-11], RECVS[-5])


def rope_tables():
    half = HD // 2
    inverse = np.exp(np.arange(half) * (-2.0 * math.log(rope_base) / HD))
    angles = np.arange(SLAB)[:, None] * inverse[None, :]
    within = np.concatenate([np.cos(angles), np.sin(angles)], axis=1)
    starts = np.tile(np.arange(4)[:, None] * SLAB * inverse[None, :], (1, 2))
    return within.astype(np.float32), np.concatenate([np.cos(starts), np.sin(starts)]).astype(np.float32)


def dot(a, b):
    return jnp.dot(a, b, preferred_element_type=F32)


def dot_nt(a, b, precision=None):
    return lax.dot_general(a, b, (((1,), (1,)), ((), ())), preferred_element_type=F32, precision=precision)


def kernel(
    act_h, gain_h, wq_h, kv_h, wo_h, ids_h, clean_h, within_h, starts_h, out,
    act, gain, ids, clean, within, starts,
    xg, held, wq, kvraw, wkv, wo, perm, cosine, sine, scale_col, own_ids,
    accq_m, acckv_m, accq_o, acckv_o, recvq, recvkv, qbuf, kv, num, den, att, sbuf, rbuf,
    sqz, sqy, sqs,
    g_send, g_recv, r_send, r_recv, s_send, s_recv, x_send, x_recv, c_send, c_recv, load_sem,
):
    col = lax.axis_index("col")
    row = lax.axis_index("row")
    seq = lax.axis_index("seq")
    z, y = col // NY, lax.rem(col, NY)
    other = 1 - row

    def plane(step):
        zz = lax.rem(z + step[0] + NZ, NZ)
        yy = lax.rem(y + step[1] + NY, NY)
        return {"col": zz * NY + yy}

    def origin(n):
        return lax.rem(z + NZ - n[0] % NZ, NZ) * NY + lax.rem(y + NY - n[1] % NY, NY)

    def along(step):
        return {"seq": lax.rem(seq + step + 4, 4)}

    sibling = {"row": other}

    barrier = pltpu.get_barrier_semaphore()
    partners = [plane(s) for s in ((1, 0), (-1, 0), (0, 1), (0, -1))] + [along(1), along(-1), sibling]
    for device in partners:
        pl.semaphore_signal(barrier, inc=1, device_id=device, device_id_type=MESH)

    def dyn(index, size):
        return pl.ds(pl.multiple_of(index * size, size), size)

    group = col // 8
    pieces = (
        (act_h, act),
        (gain_h, gain),
        (kv_h.at[:, :, dyn(group, HD)], kvraw),
        (wq_h.at[:, dyn(row, HD)], wq.at[:, pl.ds(0, HD)]),
        (wq_h.at[:, dyn(other, HD)], wq.at[:, pl.ds(HD, HD)]),
        (within_h, within),
        (starts_h, starts),
        (ids_h, ids),
        (clean_h, clean),
        (wo_h.at[dyn(row, HD), :], wo.at[pl.ds(0, HD), :]),
        (wo_h.at[dyn(other, HD), :], wo.at[pl.ds(HD, HD), :]),
    )
    loads = [pltpu.make_async_copy(src, dst, load_sem.at[i]) for i, (src, dst) in enumerate(pieces)]
    for copy in loads:
        copy.start()
    loads[0].wait()
    loads[1].wait()
    wide = act[...].astype(F32)
    xg[...] = (wide * gain[...]).astype(BF16)
    pl.semaphore_wait(barrier, len(partners))

    sent = []

    def remote(src, dst, send, recv, device):
        return pltpu.make_async_remote_copy(
            src_ref=src, dst_ref=dst, send_sem=send, recv_sem=recv, device_id=device, device_id_type=MESH
        )

    def launch(copy):
        copy.start()
        sent.append(copy)

    def landed(dst, recv, device):
        remote(dst, dst, recv, recv, device).wait_recv()

    def chunk(n, rows):
        block = pl.ds(rows.start, rows.stop - rows.start)
        if n == (0, 0):
            return xg.at[block, :]
        return held.at[slot(n), block, :]

    def send(e):
        _, above, below, step, rows = EDGES[e]
        launch(remote(chunk(above, rows), chunk(below, rows), g_send.at[e], g_recv.at[e], plane(step)))

    own_sends = next(i for i, event in enumerate(GATHER) if event[0] != "send")
    for event in GATHER[:own_sends]:
        send(event[1])

    sqz[0] = dot_nt(jnp.ones((8, CH), F32), wide * wide, lax.Precision.HIGHEST)

    def square_ring(ref, at, axis, base):
        size = ref.shape[0]
        for direction, hops in ((1, size // 2), (-1, size // 2 - 1)):
            distance = at if direction == 1 else (size - at) % size
            if distance < hops and (at == 0 or distance < size // 2):
                k = (at + direction) % size
                step = (direction, 0) if axis == 0 else (0, direction)
                launch(remote(ref.at[at], ref.at[k], s_send.at[base + k], s_recv.at[base + k], plane(step)))

    def sqz_forward(nz):
        square_ring(sqz, nz, 0, 0)

    def sqy_forward(ny):
        square_ring(sqy, ny, 1, 8)

    sqz_forward(0)

    line = lax.broadcasted_iota(jnp.int32, (2 * CH, 2 * CH), 0)
    lane = lax.broadcasted_iota(jnp.int32, (2 * CH, 2 * CH), 1)
    upper = (line >= CH).astype(jnp.int32)
    kind = jnp.where(row == 0, upper, 1 - upper)
    perm[...] = jnp.where(lane == 2 * (line - CH * upper) + kind, 1.0, 0.0).astype(BF16)
    for acc in (accq_m, acckv_m, accq_o, acckv_o):
        acc[...] = jnp.zeros_like(acc)

    apart = set()

    def compute(pair, n, last):
        if not apart:
            for copy in loads[2:5]:
                copy.wait()
        at = dyn(origin(n), CH)
        if n not in apart:
            apart.add(n)
            split = dot(perm[...], kvraw[at, :, :].reshape(2 * CH, HD)).astype(BF16)
            wkv[at, pl.ds(0, HD)] = split[:CH]
            wkv[at, pl.ds(HD, HD)] = split[CH:]
        first, rows = ROWS[pair]
        block = pl.ds(first, rows)
        x = xg[block, :] if n == (0, 0) else held[slot(n), block, :]
        theirs = dot(x, jnp.concatenate([wkv[at, pl.ds(HD, HD)], wq[at, pl.ds(HD, HD)]], axis=1))
        acckv_o[block, :] += theirs[:, :HD]
        accq_o[block, :] += theirs[:, HD:]
        if last:
            launch(remote(acckv_o.at[block, :], recvkv.at[block, :], c_send.at[8 * pair], c_recv.at[8 * pair], sibling))
        mine = dot(x, jnp.concatenate([wkv[at, pl.ds(0, HD)], wq[at, pl.ds(0, HD)]], axis=1))
        acckv_m[block, :] += mine[:, :HD]
        accq_m[block, :] += mine[:, HD:]

    def prepare():
        for copy in loads[5:9]:
            copy.wait()
        table = within[...]
        turned = pltpu.roll(table, HD // 2, 1)
        low = lax.broadcasted_iota(jnp.int32, (SLAB, HD), 1) < HD // 2
        cos_t, sin_t = jnp.where(low, table, turned), jnp.where(low, turned, table)
        cos_s, sin_s = starts[pl.ds(seq, 1), :], starts[pl.ds(seq + 4, 1), :]
        cosine[...] = cos_t * cos_s - sin_t * sin_s
        both = sin_t * cos_s + cos_t * sin_s
        sine[...] = jnp.where(low, -both, both)
        own_ids[...] = jnp.broadcast_to(ids[:, dyn(seq, SLAB)].astype(F32), (HD, SLAB)).T
        num[...] = jnp.zeros_like(num)
        den[...] = jnp.zeros_like(den)

    z_left = NZ - 1
    missing = {key: len(UP.get(key, [])) for key in NODES}
    for position, event in enumerate(GATHER):
        if position < own_sends:
            continue
        if position == FIRST_AT:
            prepare()
        if position == SQUARES_AT[0]:
            landed(sqy.at[1], s_recv.at[9], plane((0, -1)))
            sqy_forward(1)
        if position == SQUARES_AT[1]:
            landed(sqy.at[2], s_recv.at[10], plane((0, -1)))
            landed(sqy.at[3], s_recv.at[11], plane((0, 1)))
            sqs[0] = sqy[0] + sqy[1] + sqy[2] + sqy[3]
            launch(remote(sqs.at[0], sqs.at[1], c_send.at[1], c_recv.at[1], sibling))
        if position == SQUARES_AT[2]:
            landed(sqs.at[1], c_recv.at[1], sibling)
            squares = sqs[0] + sqs[1]
            scaling = lax.rsqrt(squares[:1] / D + norm_eps)
            scale_col[...] = jnp.broadcast_to(scaling, (HD, SLAB)).T
        if event[0] == "comp":
            compute(event[1], event[2], position == LAST_COMP[event[1]])
            continue
        if event[0] == "send":
            send(event[1])
            continue
        part, above, n, step, rows = EDGES[event[1]]
        landed(chunk(n, rows), g_recv.at[event[1]], plane((-step[0], -step[1])))
        missing[(part, n)] -= 1
        if missing[(part, n)]:
            continue
        if part == 1 and n[1] == 0:
            landed(sqz.at[n[0]], s_recv.at[n[0]], plane((-1, 0) if n[0] <= NZ // 2 else (1, 0)))
            sqz_forward(n[0])
            z_left -= 1
            if z_left == 0:
                total = sqz[0]
                for k in range(1, NZ):
                    total = total + sqz[k]
                sqy[0] = total
                sqy_forward(0)

    launch(remote(accq_o, recvq, c_send.at[7], c_recv.at[7], sibling))

    half = SLAB // 2
    halves = (pl.ds(0, half), pl.ds(half, half))
    is_key = (row == 0).astype(F32)
    for part in (1, 0):
        block = pl.ds(*ROWS[part])
        landed(recvkv.at[block, :], c_recv.at[8 * part], sibling)
    kv_sum = (acckv_m[...] + recvkv[...]) * scale_col[...]
    cos_kv = cosine[...] * is_key + (1.0 - is_key)
    kv[row, 0] = (kv_sum * cos_kv + pltpu.roll(kv_sum, HD // 2, 1) * (sine[...] * is_key)).astype(BF16)

    def over(source, target, part, sem, step):
        piece = halves[part]
        launch(
            remote(kv.at[row, source, piece], kv.at[row, target, piece], x_send.at[sem], x_recv.at[sem], along(step))
        )

    def arrived(target, part, sem, step):
        landed(kv.at[row, target, halves[part]], x_recv.at[sem], along(-step))

    def across(target, sem):
        launch(remote(kv.at[row, target], kv.at[row, target], c_send.at[sem], c_recv.at[sem], sibling))

    over(0, 1, 0, 0, 1)
    over(0, 3, 1, 1, -1)
    over(0, 1, 1, 2, 1)
    over(0, 3, 0, 3, -1)
    across(0, 2)

    landed(recvq, c_recv.at[7], sibling)
    q_sum = (accq_m[...] + recvq[...]) * scale_col[...]
    qbuf[...] = (q_sum * cosine[...] + pltpu.roll(q_sum, HD // 2, 1) * sine[...]).astype(BF16)
    score_scale = 1.0 / math.sqrt(HD)

    def attend(k, part=None):
        size = SLAB if part is None else half
        keys = pl.ds(0, SLAB) if part is None else halves[part]
        from_seq = lax.rem(seq + 4 - k, 4)
        place = pl.ds(pl.multiple_of(from_seq * SLAB + (part or 0) * half, half), size)
        key_ids = ids[:, place].astype(F32)
        open_to = jnp.where(clean[:, place] == 1, 1e9, key_ids)
        scores = dot_nt(qbuf[...], kv[0, k, keys, :]) * score_scale
        mine = own_ids[:, :1]
        visible = (mine >= key_ids) & (mine <= open_to)
        weights = jnp.where(visible, jnp.exp(scores), 0.0)
        share = weights[:, :HD]
        for first in range(HD, size, HD):
            share = share + weights[:, first : first + HD]
        den[...] += share
        num[...] += dot(weights.astype(BF16), kv[1, k, keys, :])

    arrived(1, 0, 0, 1)
    over(1, 2, 0, 4, 1)
    arrived(3, 1, 1, -1)
    over(3, 2, 1, 5, -1)
    landed(kv.at[other, 0], c_recv.at[2], sibling)
    arrived(1, 1, 2, 1)
    across(1, 3)
    arrived(3, 0, 3, -1)
    across(3, 4)
    attend(0)
    landed(kv.at[other, 1], c_recv.at[3], sibling)
    attend(1)
    for part, step in ((0, 1), (1, -1)):
        arrived(2, part, 4 + part, step)
        piece = kv.at[row, 2, halves[part]]
        launch(remote(piece, piece, c_send.at[5 + 4 * part], c_recv.at[5 + 4 * part], sibling))
    landed(kv.at[other, 3], c_recv.at[4], sibling)
    attend(3)
    for part in (0, 1):
        landed(kv.at[other, 2, halves[part]], c_recv.at[5 + 4 * part], sibling)
        attend(2, part)

    att[0] = (num[...] / jnp.sum(den[...], axis=1, keepdims=True)).astype(BF16)
    launch(remote(att.at[0], att.at[1], c_send.at[6], c_recv.at[6], sibling))
    for copy in loads[9:]:
        copy.wait()
    landed(att.at[1], c_recv.at[6], sibling)

    for p, n in REDUCE:
        first, rows = ROWS[p]
        block = pl.ds(first, rows)
        left = jnp.concatenate([att[0, block, :], att[1, block, :]], axis=1)
        value = dot(left, wo[:, dyn(origin(n), CH)])
        for e in DOWN.get((p, n), []):
            _, _, below, step, part = EDGES[e]
            piece = pl.ds(part.start, part.stop - part.start)
            landed(rbuf.at[slot(below), piece, :], r_recv.at[e], plane(step))
            term = rbuf[slot(below), piece, :].astype(F32)
            if part == WHOLE[p]:
                value = value + term
            elif part.start == first:
                cut = part.stop - first
                value = jnp.concatenate([value[:cut] + term, value[cut:]], axis=0)
            else:
                cut = part.start - first
                value = jnp.concatenate([value[:cut], value[cut:] + term], axis=0)
        if n == (0, 0):
            out[block, :] = value.astype(BF16)
            continue
        sbuf[slot(n), block, :] = value.astype(BF16)
        for e in UP[(p, n)]:
            _, _, _, step, part = EDGES[e]
            piece = pl.ds(part.start, part.stop - part.start)
            launch(
                remote(
                    sbuf.at[slot(n), piece, :], rbuf.at[slot(n), piece, :],
                    r_send.at[e], r_recv.at[e], plane((-step[0], -step[1])),
                )
            )

    for copy in sent:
        copy.wait_send()


def shards(activations, norm_gain, query_weight, kv_weight, out_weight, block_ids, clean_mask):
    features = query_weight.shape[0]
    length = block_ids.shape[0]
    vmem = pl.BlockSpec(memory_space=pltpu.VMEM)
    hbm = pl.BlockSpec(memory_space=pl.ANY)
    dma = pltpu.SemaphoreType.DMA
    edges = len(EDGES)
    tokens_f32 = pltpu.VMEM((SLAB, HD), F32)
    within, starts = rope_tables()
    return pl.pallas_call(
        kernel,
        out_shape=jax.ShapeDtypeStruct((SLAB, CH), BF16),
        in_specs=[hbm] * 9,
        out_specs=vmem,
        scratch_shapes=[
            pltpu.VMEM((SLAB, CH), BF16),
            pltpu.VMEM((1, CH), F32),
            pltpu.VMEM((1, length), jnp.int32),
            pltpu.VMEM((1, length), jnp.int32),
            tokens_f32,
            pltpu.VMEM((8, HD), F32),
            pltpu.VMEM((SLAB, CH), BF16),
            pltpu.VMEM((NZ * NY, SLAB, CH), BF16),
            pltpu.VMEM((features, 2 * HD), BF16),
            pltpu.VMEM((features, 2, HD), BF16),
            pltpu.VMEM((features, 2 * HD), BF16),
            pltpu.VMEM((2 * HD, out_weight.shape[1]), BF16),
            pltpu.VMEM((2 * CH, 2 * CH), BF16),
            tokens_f32, tokens_f32, tokens_f32, tokens_f32,
            tokens_f32, tokens_f32, tokens_f32, tokens_f32,
            tokens_f32, tokens_f32,
            pltpu.VMEM((SLAB, HD), BF16),
            pltpu.VMEM((2, 4, SLAB, HD), BF16),
            tokens_f32, tokens_f32,
            pltpu.VMEM((2, SLAB, HD), BF16),
            pltpu.VMEM((NZ * NY, SLAB, CH), BF16),
            pltpu.VMEM((NZ * NY, SLAB, CH), BF16),
            pltpu.VMEM((NZ, 8, SLAB), F32),
            pltpu.VMEM((NY, 8, SLAB), F32),
            pltpu.VMEM((2, 8, SLAB), F32),
            dma((edges,)), dma((edges,)), dma((edges,)), dma((edges,)),
            dma((12,)), dma((12,)), dma((6,)), dma((6,)), dma((10,)), dma((10,)), dma((11,)),
        ],
        compiler_params=pltpu.CompilerParams(
            collective_id=0, has_side_effects=True, vmem_limit_bytes=VMEM_LIMIT
        ),
        name="layer",
    )(
        activations,
        norm_gain.reshape(1, CH),
        query_weight,
        kv_weight,
        out_weight,
        block_ids.reshape(1, length),
        clean_mask.reshape(1, length),
        jnp.asarray(within),
        jnp.asarray(starts),
    )


def solution(mesh):
    placed = (
        P("seq", ("row", "col")),
        P(("row", "col")),
        P("row", "col"),
        P("row", None, None),
        P("col", "row"),
        P(),
        P(),
    )
    return jax.shard_map(
        shards, mesh=mesh, in_specs=placed, out_specs=P("seq", ("row", "col")), check_vma=False
    )
```

```python
import heapq
import math
import random

import jax
import jax.numpy as jnp
import numpy as np
from jax import lax
from jax.experimental import pallas as pl
from jax.experimental.pallas import tpu as pltpu
from jax.sharding import PartitionSpec as P

D = 16384
HD = 128
QH = 64
KVH = 4
rope_base = 500000.0
norm_eps = 1e-05

MESH = pl.DeviceIdType.MESH
VMEM_LIMIT = 63 * 1024 * 1024
F32 = jnp.float32
BF16 = jnp.bfloat16

NZ, NY = 8, 4
SLAB = 512
SPLIT = 208
PARTS = ((0, SPLIT, True), (SPLIT, SLAB - SPLIT, False))
ROWS = tuple(part[:2] for part in PARTS)
CH = 256


def norm(n):
    return (n[0] % NZ, n[1] % NY)


def slot(n):
    return (n[0] % NZ) * NY + n[1] % NY


HOP_US = 1.5
COMP_US = 0.3
LOADED_US = 8.0
HALVED = True

HALVES = tuple(
    (slice(first, first + (rows // 32 + rows % 32 // 16) * 16), slice(first + (rows // 32 + rows % 32 // 16) * 16, first + rows))
    for first, rows in ROWS
)
WHOLE = tuple(slice(first, first + rows) for first, rows in ROWS)


def make_tree(part, y_first):
    edges = []

    def ring(start, axis, size, way, halved):
        for direction, hops in ((way, size // 2), (-way, size // 2 - 1)):
            at = start
            for hop in range(1, size // 2 + 1):
                step = (direction, 0) if axis == 0 else (0, direction)
                child = norm((at[0] + step[0], at[1] + step[1]))
                far = hop == size // 2
                if far and halved:
                    edges.append((at, child, step, HALVES[part][direction == way]))
                elif hop <= hops:
                    edges.append((at, child, step, WHOLE[part]))
                at = child

    root = (0, 0)
    if y_first:
        ring(root, 1, NY, 1, HALVED)
        for ny in range(NY):
            ring((0, ny), 0, NZ, 1 if ny % 2 == 0 else -1, False)
    else:
        ring(root, 0, NZ, -1, HALVED)
        for nz in range(NZ):
            ring((nz, 0), 1, NY, -1 if nz % 2 == 0 else 1, False)
    return edges


EDGES = [(part,) + edge for part, spec in enumerate(PARTS) for edge in make_tree(part, spec[2])]
DOWN, UP = {}, {}
for number, edge in enumerate(EDGES):
    DOWN.setdefault((edge[0], edge[1]), []).append(number)
    UP.setdefault((edge[0], edge[2]), []).append(number)
NODES = [(part, (nz, ny)) for part in range(len(PARTS)) for nz in range(NZ) for ny in range(NY)]


def height(key):
    return max([1 + height((key[0], EDGES[e][2])) for e in DOWN.get(key, [])], default=0)


def depth(key):
    return max([1 + depth((key[0], EDGES[e][1])) for e in UP.get(key, [])], default=0)


DEPTH = {key: depth(key) for key in NODES}
for key in DOWN:
    DOWN[key].sort(key=lambda e: -height((EDGES[e][0], EDGES[e][2])))


def link_us(e):
    rows = EDGES[e][4]
    return (rows.stop - rows.start) * CH * 2 * 2 / 97e3


def tail_down(key):
    return max([link_us(e) + HOP_US + tail_down((key[0], EDGES[e][2])) for e in DOWN.get(key, [])], default=0.0)


def tail_up(key):
    return max([link_us(e) + HOP_US + 0.3 + tail_up((key[0], EDGES[e][1])) for e in UP.get(key, [])], default=0.0)


def plan_gather(backlog=1.0):
    rank = [tail_down((edge[0], edge[2])) for edge in EDGES]
    free, arrivals, events = {}, [], []
    pending = [e for part in (0, 1) for e in DOWN[(part, (0, 0))]]
    missing = {key: len(UP.get(key, [])) for key in NODES}
    ready = [(0, (0, 0)), (1, (0, 0))]
    t = 0.0
    while arrivals or ready or pending:
        able = [e for e in pending if free.get(EDGES[e][3], 0.0) - t < backlog]
        if able:
            e = max(able, key=lambda e: rank[e])
            pending.remove(e)
            step = EDGES[e][3]
            free[step] = max(t, free.get(step, 0.0)) + link_us(e)
            heapq.heappush(arrivals, (free[step] + HOP_US, e))
            events.append(("send", e))
            t += 0.01
        elif arrivals and arrivals[0][0] <= t:
            _, e = heapq.heappop(arrivals)
            events.append(("recv", e))
            t += 0.04
            key = (EDGES[e][0], EDGES[e][2])
            missing[key] -= 1
            if missing[key] == 0:
                pending += DOWN.get(key, [])
                ready.append(key)
        elif ready and t >= LOADED_US:
            events.append(("comp",) + ready.pop(0))
            t += COMP_US
        else:
            nexts = [arrivals[0][0]] if arrivals else []
            if t < LOADED_US:
                nexts.append(LOADED_US)
            if pending:
                nexts.append(min(free[EDGES[e][3]] for e in pending) - backlog + 0.001)
            t = max(t + 0.001, min(nexts))
    return events, t


def plan_reduce(backlog=2.0, jitter=0.5, seed=1):
    draw = random.Random(seed)
    rank = {key: tail_up(key) + jitter * draw.random() for key in NODES}
    free, arrivals, order = {}, [], []
    missing = {key: len(DOWN.get(key, [])) for key in NODES}
    ready = [key for key in NODES if missing[key] == 0]
    t = 0.0

    def behind(key):
        return max(free.get(EDGES[e][3], 0.0) for e in UP[key]) - t

    while arrivals or ready:
        while arrivals and arrivals[0][0] <= t:
            _, e = heapq.heappop(arrivals)
            above = (EDGES[e][0], EDGES[e][1])
            missing[above] -= 1
            if missing[above] == 0:
                ready.append(above)
        able = [key for key in ready if key in UP and behind(key) < backlog]
        roots = [key for key in ready if key not in UP]
        if able:
            key = max(able, key=lambda key: rank[key] - 0.5 * max(0.0, behind(key)))
        elif roots:
            key = roots[0]
        else:
            nexts = [arrivals[0][0]] if arrivals else []
            if ready:
                nexts.append(min(behind(key) for key in ready) + t - backlog + 0.001)
            t = max(t + 0.001, min(nexts))
            continue
        ready.remove(key)
        order.append(key)
        t += 0.1 + 0.2 * ROWS[key[0]][1] / CH
        for e in UP.get(key, []):
            step = EDGES[e][3]
            free[step] = max(t, free.get(step, 0.0)) + link_us(e)
            heapq.heappush(arrivals, (free[step] + HOP_US, e))
    return order, t


GATHER, GATHER_US = plan_gather()
REDUCE, REDUCE_US = plan_reduce()
LAST_COMP = [max(i for i, event in enumerate(GATHER) if event[:2] == ("comp", part)) for part in (0, 1)]
RECVS = [i for i, event in enumerate(GATHER) if event[0] == "recv"]
FIRST_AT, SQUARES_AT = RECVS[4], (RECVS[-18], RECVS[-11], RECVS[-5])


def rope_tables():
    half = HD // 2
    inverse = np.exp(np.arange(half) * (-2.0 * math.log(rope_base) / HD))
    angles = np.arange(SLAB)[:, None] * inverse[None, :]
    within = np.concatenate([np.cos(angles), np.sin(angles)], axis=1)
    starts = np.tile(np.arange(4)[:, None] * SLAB * inverse[None, :], (1, 2))
    return within.astype(np.float32), np.concatenate([np.cos(starts), np.sin(starts)]).astype(np.float32)


def dot(a, b):
    return jnp.dot(a, b, preferred_element_type=F32)


def dot_nt(a, b, precision=None):
    return lax.dot_general(a, b, (((1,), (1,)), ((), ())), preferred_element_type=F32, precision=precision)


def kernel(
    act_h, gain_h, wq_h, kv_h, wo_h, ids_h, clean_h, within_h, starts_h, out,
    act, gain, ids, clean, within, starts,
    xg, held, wq, kvraw, wkv, wo, perm, cosine, sine, scale_col, own_ids,
    accq_m, acckv_m, accq_o, acckv_o, recvq, recvkv, qbuf, kv, num, den, att, sbuf, rbuf,
    sqz, sqy, sqs,
    g_send, g_recv, r_send, r_recv, s_send, s_recv, x_send, x_recv, c_send, c_recv, load_sem,
):
    col = lax.axis_index("col")
    row = lax.axis_index("row")
    seq = lax.axis_index("seq")
    z, y = col // NY, lax.rem(col, NY)
    other = 1 - row

    def plane(step):
        zz = lax.rem(z + step[0] + NZ, NZ)
        yy = lax.rem(y + step[1] + NY, NY)
        return {"col": zz * NY + yy}

    def origin(n):
        return lax.rem(z + NZ - n[0] % NZ, NZ) * NY + lax.rem(y + NY - n[1] % NY, NY)

    def along(step):
        return {"seq": lax.rem(seq + step + 4, 4)}

    sibling = {"row": other}

    barrier = pltpu.get_barrier_semaphore()
    partners = [plane(s) for s in ((1, 0), (-1, 0), (0, 1), (0, -1))] + [along(1), along(-1), sibling]
    for device in partners:
        pl.semaphore_signal(barrier, inc=1, device_id=device, device_id_type=MESH)

    def dyn(index, size):
        return pl.ds(pl.multiple_of(index * size, size), size)

    group = col // 8
    pieces = (
        (act_h, act),
        (gain_h, gain),
        (kv_h.at[:, :, dyn(group, HD)], kvraw),
        (wq_h.at[:, dyn(row, HD)], wq.at[:, pl.ds(0, HD)]),
        (wq_h.at[:, dyn(other, HD)], wq.at[:, pl.ds(HD, HD)]),
        (within_h, within),
        (starts_h, starts),
        (ids_h, ids),
        (clean_h, clean),
        (wo_h.at[dyn(row, HD), :], wo.at[pl.ds(0, HD), :]),
        (wo_h.at[dyn(other, HD), :], wo.at[pl.ds(HD, HD), :]),
    )
    loads = [pltpu.make_async_copy(src, dst, load_sem.at[i]) for i, (src, dst) in enumerate(pieces)]
    for copy in loads:
        copy.start()
    loads[0].wait()
    loads[1].wait()
    wide = act[...].astype(F32)
    xg[...] = (wide * gain[...]).astype(BF16)
    pl.semaphore_wait(barrier, len(partners))

    sent = []

    def remote(src, dst, send, recv, device):
        return pltpu.make_async_remote_copy(
            src_ref=src, dst_ref=dst, send_sem=send, recv_sem=recv, device_id=device, device_id_type=MESH
        )

    def launch(copy):
        copy.start()
        sent.append(copy)

    def landed(dst, recv, device):
        remote(dst, dst, recv, recv, device).wait_recv()

    def chunk(n, rows):
        block = pl.ds(rows.start, rows.stop - rows.start)
        if n == (0, 0):
            return xg.at[block, :]
        return held.at[slot(n), block, :]

    def send(e):
        _, above, below, step, rows = EDGES[e]
        launch(remote(chunk(above, rows), chunk(below, rows), g_send.at[e], g_recv.at[e], plane(step)))

    own_sends = next(i for i, event in enumerate(GATHER) if event[0] != "send")
    for event in GATHER[:own_sends]:
        send(event[1])

    sqz[0] = dot_nt(jnp.ones((8, CH), F32), wide * wide, lax.Precision.HIGHEST)

    def square_ring(ref, at, axis, base):
        size = ref.shape[0]
        for direction, hops in ((1, size // 2), (-1, size // 2 - 1)):
            distance = at if direction == 1 else (size - at) % size
            if distance < hops and (at == 0 or distance < size // 2):
                k = (at + direction) % size
                step = (direction, 0) if axis == 0 else (0, direction)
                launch(remote(ref.at[at], ref.at[k], s_send.at[base + k], s_recv.at[base + k], plane(step)))

    def sqz_forward(nz):
        square_ring(sqz, nz, 0, 0)

    def sqy_forward(ny):
        square_ring(sqy, ny, 1, 8)

    sqz_forward(0)

    line = lax.broadcasted_iota(jnp.int32, (2 * CH, 2 * CH), 0)
    lane = lax.broadcasted_iota(jnp.int32, (2 * CH, 2 * CH), 1)
    upper = (line >= CH).astype(jnp.int32)
    kind = jnp.where(row == 0, upper, 1 - upper)
    perm[...] = jnp.where(lane == 2 * (line - CH * upper) + kind, 1.0, 0.0).astype(BF16)
    for acc in (accq_m, acckv_m, accq_o, acckv_o):
        acc[...] = jnp.zeros_like(acc)

    apart = set()

    def compute(pair, n, last):
        if not apart:
            for copy in loads[2:5]:
                copy.wait()
        at = dyn(origin(n), CH)
        if n not in apart:
            apart.add(n)
            split = dot(perm[...], kvraw[at, :, :].reshape(2 * CH, HD)).astype(BF16)
            wkv[at, pl.ds(0, HD)] = split[:CH]
            wkv[at, pl.ds(HD, HD)] = split[CH:]
        first, rows = ROWS[pair]
        block = pl.ds(first, rows)
        x = xg[block, :] if n == (0, 0) else held[slot(n), block, :]
        theirs = dot(x, jnp.concatenate([wkv[at, pl.ds(HD, HD)], wq[at, pl.ds(HD, HD)]], axis=1))
        acckv_o[block, :] += theirs[:, :HD]
        accq_o[block, :] += theirs[:, HD:]
        if last:
            launch(remote(acckv_o.at[block, :], recvkv.at[block, :], c_send.at[8 * pair], c_recv.at[8 * pair], sibling))
        mine = dot(x, jnp.concatenate([wkv[at, pl.ds(0, HD)], wq[at, pl.ds(0, HD)]], axis=1))
        acckv_m[block, :] += mine[:, :HD]
        accq_m[block, :] += mine[:, HD:]

    def prepare():
        for copy in loads[5:9]:
            copy.wait()
        table = within[...]
        turned = pltpu.roll(table, HD // 2, 1)
        low = lax.broadcasted_iota(jnp.int32, (SLAB, HD), 1) < HD // 2
        cos_t, sin_t = jnp.where(low, table, turned), jnp.where(low, turned, table)
        cos_s, sin_s = starts[pl.ds(seq, 1), :], starts[pl.ds(seq + 4, 1), :]
        cosine[...] = cos_t * cos_s - sin_t * sin_s
        both = sin_t * cos_s + cos_t * sin_s
        sine[...] = jnp.where(low, -both, both)
        own_ids[...] = jnp.broadcast_to(ids[:, dyn(seq, SLAB)].astype(F32), (HD, SLAB)).T
        num[...] = jnp.zeros_like(num)
        den[...] = jnp.zeros_like(den)

    z_left = NZ - 1
    missing = {key: len(UP.get(key, [])) for key in NODES}
    for position, event in enumerate(GATHER):
        if position < own_sends:
            continue
        if position == FIRST_AT:
            prepare()
        if position == SQUARES_AT[0]:
            landed(sqy.at[1], s_recv.at[9], plane((0, -1)))
            sqy_forward(1)
        if position == SQUARES_AT[1]:
            landed(sqy.at[2], s_recv.at[10], plane((0, -1)))
            landed(sqy.at[3], s_recv.at[11], plane((0, 1)))
            sqs[0] = sqy[0] + sqy[1] + sqy[2] + sqy[3]
            launch(remote(sqs.at[0], sqs.at[1], c_send.at[1], c_recv.at[1], sibling))
        if position == SQUARES_AT[2]:
            landed(sqs.at[1], c_recv.at[1], sibling)
            squares = sqs[0] + sqs[1]
            scaling = lax.rsqrt(squares[:1] / D + norm_eps)
            scale_col[...] = jnp.broadcast_to(scaling, (HD, SLAB)).T
        if event[0] == "comp":
            compute(event[1], event[2], position == LAST_COMP[event[1]])
            continue
        if event[0] == "send":
            send(event[1])
            continue
        part, above, n, step, rows = EDGES[event[1]]
        landed(chunk(n, rows), g_recv.at[event[1]], plane((-step[0], -step[1])))
        missing[(part, n)] -= 1
        if missing[(part, n)]:
            continue
        if part == 1 and n[1] == 0:
            landed(sqz.at[n[0]], s_recv.at[n[0]], plane((-1, 0) if n[0] <= NZ // 2 else (1, 0)))
            sqz_forward(n[0])
            z_left -= 1
            if z_left == 0:
                total = sqz[0]
                for k in range(1, NZ):
                    total = total + sqz[k]
                sqy[0] = total
                sqy_forward(0)

    launch(remote(accq_o, recvq, c_send.at[7], c_recv.at[7], sibling))

    half = SLAB // 2
    halves = (pl.ds(0, half), pl.ds(half, half))
    is_key = (row == 0).astype(F32)
    for part in (1, 0):
        block = pl.ds(*ROWS[part])
        landed(recvkv.at[block, :], c_recv.at[8 * part], sibling)
    kv_sum = (acckv_m[...] + recvkv[...]) * scale_col[...]
    cos_kv = cosine[...] * is_key + (1.0 - is_key)
    kv[row, 0] = (kv_sum * cos_kv + pltpu.roll(kv_sum, HD // 2, 1) * (sine[...] * is_key)).astype(BF16)

    def over(source, target, part, sem, step):
        piece = halves[part]
        launch(
            remote(kv.at[row, source, piece], kv.at[row, target, piece], x_send.at[sem], x_recv.at[sem], along(step))
        )

    def arrived(target, part, sem, step):
        landed(kv.at[row, target, halves[part]], x_recv.at[sem], along(-step))

    def across(target, sem):
        launch(remote(kv.at[row, target], kv.at[row, target], c_send.at[sem], c_recv.at[sem], sibling))

    over(0, 1, 0, 0, 1)
    over(0, 3, 1, 1, -1)
    over(0, 1, 1, 2, 1)
    over(0, 3, 0, 3, -1)
    across(0, 2)

    landed(recvq, c_recv.at[7], sibling)
    q_sum = (accq_m[...] + recvq[...]) * scale_col[...]
    qbuf[...] = (q_sum * cosine[...] + pltpu.roll(q_sum, HD // 2, 1) * sine[...]).astype(BF16)
    score_scale = 1.0 / math.sqrt(HD)

    def attend(k, part=None):
        size = SLAB if part is None else half
        keys = pl.ds(0, SLAB) if part is None else halves[part]
        from_seq = lax.rem(seq + 4 - k, 4)
        place = pl.ds(pl.multiple_of(from_seq * SLAB + (part or 0) * half, half), size)
        key_ids = ids[:, place].astype(F32)
        open_to = jnp.where(clean[:, place] == 1, 1e9, key_ids)
        scores = dot_nt(qbuf[...], kv[0, k, keys, :]) * score_scale
        mine = own_ids[:, :1]
        visible = (mine >= key_ids) & (mine <= open_to)
        weights = jnp.where(visible, jnp.exp(scores), 0.0)
        share = weights[:, :HD]
        for first in range(HD, size, HD):
            share = share + weights[:, first : first + HD]
        den[...] += share
        num[...] += dot(weights.astype(BF16), kv[1, k, keys, :])

    arrived(1, 0, 0, 1)
    over(1, 2, 0, 4, 1)
    arrived(3, 1, 1, -1)
    over(3, 2, 1, 5, -1)
    landed(kv.at[other, 0], c_recv.at[2], sibling)
    arrived(1, 1, 2, 1)
    across(1, 3)
    arrived(3, 0, 3, -1)
    across(3, 4)
    attend(0)
    landed(kv.at[other, 1], c_recv.at[3], sibling)
    attend(1)
    for part, step in ((0, 1), (1, -1)):
        arrived(2, part, 4 + part, step)
        piece = kv.at[row, 2, halves[part]]
        launch(remote(piece, piece, c_send.at[5 + 4 * part], c_recv.at[5 + 4 * part], sibling))
    landed(kv.at[other, 3], c_recv.at[4], sibling)
    attend(3)
    for part in (0, 1):
        landed(kv.at[other, 2, halves[part]], c_recv.at[5 + 4 * part], sibling)
        attend(2, part)

    lead = REDUCE[0][0]
    for part in (lead, 1 - lead):
        block = pl.ds(*ROWS[part])
        att[0, block, :] = (num[block, :] / jnp.sum(den[block, :], axis=1, keepdims=True)).astype(BF16)
        k = 6 + 4 * part
        launch(remote(att.at[0, block, :], att.at[1, block, :], c_send.at[k], c_recv.at[k], sibling))
    for copy in loads[9:]:
        copy.wait()
    attended = set()

    for p, n in REDUCE:
        first, rows = ROWS[p]
        block = pl.ds(first, rows)
        if p not in attended:
            attended.add(p)
            landed(att.at[1, block, :], c_recv.at[6 + 4 * p], sibling)
        left = jnp.concatenate([att[0, block, :], att[1, block, :]], axis=1)
        value = dot(left, wo[:, dyn(origin(n), CH)])
        for e in DOWN.get((p, n), []):
            _, _, below, step, part = EDGES[e]
            piece = pl.ds(part.start, part.stop - part.start)
            landed(rbuf.at[slot(below), piece, :], r_recv.at[e], plane(step))
            term = rbuf[slot(below), piece, :].astype(F32)
            if part == WHOLE[p]:
                value = value + term
            elif part.start == first:
                cut = part.stop - first
                value = jnp.concatenate([value[:cut] + term, value[cut:]], axis=0)
            else:
                cut = part.start - first
                value = jnp.concatenate([value[:cut], value[cut:] + term], axis=0)
        if n == (0, 0):
            out[block, :] = value.astype(BF16)
            continue
        sbuf[slot(n), block, :] = value.astype(BF16)
        for e in UP[(p, n)]:
            _, _, _, step, part = EDGES[e]
            piece = pl.ds(part.start, part.stop - part.start)
            launch(
                remote(
                    sbuf.at[slot(n), piece, :], rbuf.at[slot(n), piece, :],
                    r_send.at[e], r_recv.at[e], plane((-step[0], -step[1])),
                )
            )

    for copy in sent:
        copy.wait_send()


def shards(activations, norm_gain, query_weight, kv_weight, out_weight, block_ids, clean_mask):
    features = query_weight.shape[0]
    length = block_ids.shape[0]
    vmem = pl.BlockSpec(memory_space=pltpu.VMEM)
    hbm = pl.BlockSpec(memory_space=pl.ANY)
    dma = pltpu.SemaphoreType.DMA
    edges = len(EDGES)
    tokens_f32 = pltpu.VMEM((SLAB, HD), F32)
    within, starts = rope_tables()
    return pl.pallas_call(
        kernel,
        out_shape=jax.ShapeDtypeStruct((SLAB, CH), BF16),
        in_specs=[hbm] * 9,
        out_specs=vmem,
        scratch_shapes=[
            pltpu.VMEM((SLAB, CH), BF16),
            pltpu.VMEM((1, CH), F32),
            pltpu.VMEM((1, length), jnp.int32),
            pltpu.VMEM((1, length), jnp.int32),
            tokens_f32,
            pltpu.VMEM((8, HD), F32),
            pltpu.VMEM((SLAB, CH), BF16),
            pltpu.VMEM((NZ * NY, SLAB, CH), BF16),
            pltpu.VMEM((features, 2 * HD), BF16),
            pltpu.VMEM((features, 2, HD), BF16),
            pltpu.VMEM((features, 2 * HD), BF16),
            pltpu.VMEM((2 * HD, out_weight.shape[1]), BF16),
            pltpu.VMEM((2 * CH, 2 * CH), BF16),
            tokens_f32, tokens_f32, tokens_f32, tokens_f32,
            tokens_f32, tokens_f32, tokens_f32, tokens_f32,
            tokens_f32, tokens_f32,
            pltpu.VMEM((SLAB, HD), BF16),
            pltpu.VMEM((2, 4, SLAB, HD), BF16),
            tokens_f32, tokens_f32,
            pltpu.VMEM((2, SLAB, HD), BF16),
            pltpu.VMEM((NZ * NY, SLAB, CH), BF16),
            pltpu.VMEM((NZ * NY, SLAB, CH), BF16),
            pltpu.VMEM((NZ, 8, SLAB), F32),
            pltpu.VMEM((NY, 8, SLAB), F32),
            pltpu.VMEM((2, 8, SLAB), F32),
            dma((edges,)), dma((edges,)), dma((edges,)), dma((edges,)),
            dma((12,)), dma((12,)), dma((6,)), dma((6,)), dma((11,)), dma((11,)), dma((11,)),
        ],
        compiler_params=pltpu.CompilerParams(
            collective_id=0, has_side_effects=True, vmem_limit_bytes=VMEM_LIMIT
        ),
        name="layer",
    )(
        activations,
        norm_gain.reshape(1, CH),
        query_weight,
        kv_weight,
        out_weight,
        block_ids.reshape(1, length),
        clean_mask.reshape(1, length),
        jnp.asarray(within),
        jnp.asarray(starts),
    )


def solution(mesh):
    placed = (
        P("seq", ("row", "col")),
        P(("row", "col")),
        P("row", "col"),
        P("row", None, None),
        P("col", "row"),
        P(),
        P(),
    )
    return jax.shard_map(
        shards, mesh=mesh, in_specs=placed, out_specs=P("seq", ("row", "col")), check_vma=False
    )
```
